256 devices in a mesh: row: 32 (over z, x), col: 8 (over y, core).
Axes of the slice: x: 4, y: 4, z: 8, core: 2. Of those that a mesh axis runs over, the one named last changes fastest.
Arguments:
- block_input: bfloat16 [1, 256, 256, 512], P(None, 'row', 'col'), may hold values from -6 to 6
- kernel_three: float32 [7, 7, 512], replicated, may hold values from -0.875 to 0.875
- gain_three: float32 [512], replicated, may hold values from 0.1 to 1.9
- expand_weight: bfloat16 [512, 2048], replicated, may hold values from -0.25 to 0.25
- project_weight: bfloat16 [2048, 512], replicated, may hold values from -0.125 to 0.125
- layer_scale: float32 [512], replicated, may hold values from 0.1 to 1
- merge_gain: float32 [512], replicated, may hold values from 0.1 to 1.9
- patch_weight: bfloat16 [2048, 1024], replicated, may hold values from -0.125 to 0.125
- kernel_four: float32 [7, 7, 1024], replicated, may hold values from -0.875 to 0.875
- gain_four: float32 [1024], replicated, may hold values from 0.1 to 1.9
- normed_cotangent: bfloat16 [1, 128, 128, 1024], P(None, 'row', 'col'), may hold values from -6 to 6
- residual_cotangent: bfloat16 [1, 128, 128, 1024], P(None, 'row', 'col'), may hold values from -6 to 6
Outputs:
- input_grad: bfloat16 [1, 256, 256, 512], P(None, 'row', 'col')
- kernel_three_grad: float32 [7, 7, 512], replicated
- gain_three_grad: float32 [512], replicated
- expand_grad: float32 [512, 2048], P('row')
- project_grad: float32 [2048, 512], P('row')
- scale_grad: float32 [512], replicated
- merge_gain_grad: float32 [512], replicated
- patch_grad: float32 [2048, 1024], P('row')
- kernel_four_grad: float32 [7, 7, 1024], replicated
- gain_four_grad: float32 [1024], replicated
The draws below stay inside these ranges and needn't reach their ends.
All inputs are finite; a program needn't handle non-finite values.
Results may differ from the reference program's by a relative error of at most 0.03.
Values may be sent and summed in bfloat16 or wider, within the bound.
A program may use at most 128 MiB of HBM per device.

```python
import math
import jax
import jax.numpy as jnp
from jax import lax

D3 = 512
FF3 = 2048
D4 = 1024
BATCH = 1
R3 = 8
H3 = 256
W3 = 256
H4 = 128
W4 = 128


def block_scale(key, shape, shards, low, top_value):
    factor_of = 1.0
    for dim, blocks in shards:
        heights = jax.random.uniform(jax.random.fold_in(jax.random.fold_in(key, 6), dim), (blocks,), jnp.float32, low / len(shards), top_value / len(shards))
        factor_of = factor_of * jnp.repeat(jnp.exp(heights), shape[dim] // blocks).reshape((-1,) + (1,) * (len(shape) - 1 - dim))
    return factor_of


def centred(rng, dims, scale, reach, split=(), dtype=jnp.bfloat16):
    result = scale * jax.random.normal(rng, dims, jnp.float32)
    if split:
        result = result * block_scale(rng, dims, split, -0.22, 0.18)
    return jnp.clip(result, -reach, reach).astype(dtype)


def setup_inputs(seed: int = 0) -> dict:
    seeds = jax.random.split(jax.random.key(seed), 13)
    return {
        "block_input": centred(seeds[0], (BATCH, H3, W3, D3), 1.0, 6.0, ((1, 32), (2, 8))),
        "kernel_three": centred(seeds[1], (7, 7, D3), 49 ** -0.5, 0.875, (), jnp.float32),
        "gain_three": jnp.clip(1.0 + 0.18 * jax.random.normal(seeds[2], (D3,), jnp.float32), 0.1, 1.9),
        "expand_weight": centred(seeds[3], (D3, FF3), D3 ** -0.5, 0.25),
        "project_weight": centred(seeds[4], (FF3, D3), FF3 ** -0.5, 0.125),
        "layer_scale": jnp.clip(jnp.exp(jax.random.uniform(seeds[5], (D3,), jnp.float32, math.log(0.1), math.log(1.0))), 0.1, 1.0),
        "merge_gain": jnp.clip(1.0 + 0.18 * jax.random.normal(seeds[6], (D3,), jnp.float32), 0.1, 1.9),
        "patch_weight": centred(seeds[7], (4 * D3, D4), (4 * D3) ** -0.5, 0.125),
        "kernel_four": centred(seeds[8], (7, 7, D4), 49 ** -0.5, 0.875, (), jnp.float32),
        "gain_four": jnp.clip(1.0 + 0.18 * jax.random.normal(seeds[9], (D4,), jnp.float32), 0.1, 1.9),
        "normed_cotangent": centred(seeds[10], (BATCH, H4, W4, D4), 1.0, 6.0, ((1, 32), (2, 8))),
        "residual_cotangent": centred(seeds[11], (BATCH, H4, W4, D4), 1.0, 6.0, ((1, 32), (2, 8))),
    }


EPSILON = 1e-06

def conv_forward(values, kernel):
    extent = values.shape
    padded = jnp.pad(values, ((0, 0), (3, 3), (3, 3), (0, 0)))
    running = jnp.zeros(extent, jnp.float32)
    for vertical in range(7):
        for lateral in range(7):
            window = padded[:, vertical:vertical + extent[1], lateral:lateral + extent[2], :]
            running = running + window.astype(jnp.float32) * kernel[vertical, lateral]
    return running

def conv_transpose(values, kernel):
    extent = values.shape
    padded = jnp.pad(values, ((0, 0), (3, 3), (3, 3), (0, 0)))
    running = jnp.zeros(extent, jnp.float32)
    for vertical in range(7):
        for lateral in range(7):
            window = padded[:, 6 - vertical:6 - vertical + extent[1], 6 - lateral:6 - lateral + extent[2], :]
            running = running + window.astype(jnp.float32) * kernel[vertical, lateral]
    return running

def conv_weight_grad(values, grads):
    extent = values.shape
    padded = jnp.pad(values, ((0, 0), (3, 3), (3, 3), (0, 0)))
    grads_wide = grads.astype(jnp.float32)
    pieces = []
    for vertical in range(7):
        for lateral in range(7):
            window = padded[:, vertical:vertical + extent[1], lateral:lateral + extent[2], :]
            pieces.append(lax.optimization_barrier(jnp.sum(window.astype(jnp.float32) * grads_wide, axis=(0, 1, 2))))
    return jnp.stack(pieces).reshape(7, 7, extent[3])

def normalize(values):
    mean_value = lax.optimization_barrier(jnp.mean(values, axis=-1, keepdims=True))
    square = lax.optimization_barrier(jnp.mean(values * values, axis=-1, keepdims=True))
    inverse = lax.rsqrt(square - mean_value * mean_value + EPSILON)
    return ((values - mean_value) * inverse, inverse)

def normalize_back(grads, unit_values, inverse):
    return (grads - lax.optimization_barrier(jnp.mean(grads, axis=-1, keepdims=True)) - unit_values * lax.optimization_barrier(jnp.mean(grads * unit_values, axis=-1, keepdims=True))) * inverse

def gelu_slope(values):
    cumulative = 0.5 * (1.0 + jax.scipy.special.erf(values * (1.0 / math.sqrt(2.0))))
    return cumulative + values * jnp.exp(-0.5 * values * values) * (1.0 / math.sqrt(2.0 * math.pi))

def reference(block_input, kernel_three, gain_three, expand_weight, project_weight, layer_scale, merge_gain, patch_weight, kernel_four, gain_four, normed_cotangent, residual_cotangent):
    crop_count, height, breadth, channels = block_input.shape
    hidden_width = expand_weight.shape[1]
    wide_channels = patch_weight.shape[1]
    half_height = height // 2
    half_breadth = breadth // 2
    scale_three = 1.0 / math.sqrt(crop_count * height * breadth)
    scale_four = 1.0 / math.sqrt(crop_count * half_height * half_breadth)
    mixed = conv_forward(block_input, kernel_three)
    groups = crop_count * height // R3
    mixed_blocks = mixed.reshape(groups, R3 * breadth, channels)
    input_blocks = block_input.reshape(groups, R3 * breadth, channels)

    def forward_block(mixed_block):
        unit_mixed, inverse_mixed = normalize(mixed_block)
        normed = (unit_mixed * gain_three).astype(jnp.bfloat16)
        upward = jnp.dot(normed, expand_weight, preferred_element_type=jnp.float32)
        hidden = jax.nn.gelu(upward, approximate=False).astype(jnp.bfloat16)
        branch = jnp.dot(hidden, project_weight, preferred_element_type=jnp.float32)
        return (unit_mixed, inverse_mixed, normed, upward, hidden, branch)

    def branch_only(mixed_block):
        return forward_block(mixed_block)[5]
    branches = lax.map(branch_only, mixed_blocks)
    summed = (input_blocks.astype(jnp.float32) + layer_scale * branches).reshape(crop_count, height, breadth, channels)
    unit_summed, inverse_summed = normalize(summed)
    merged = (unit_summed * merge_gain).astype(jnp.bfloat16)
    patches = merged.reshape(crop_count, half_height, 2, half_breadth, 2, channels)
    patches = patches.transpose(0, 1, 3, 2, 4, 5).reshape(crop_count * half_height * half_breadth, 4 * channels)
    section_in = jnp.dot(patches, patch_weight, preferred_element_type=jnp.float32).astype(jnp.bfloat16)
    section_in = section_in.reshape(crop_count, half_height, half_breadth, wide_channels)
    mixed_four = conv_forward(section_in, kernel_four)
    unit_four, inverse_four = normalize(mixed_four)
    cot_four = normed_cotangent.astype(jnp.float32)
    gain_four_grad = scale_four * lax.optimization_barrier(jnp.sum(cot_four * unit_four, axis=(0, 1, 2)))
    grad_four = normalize_back(cot_four * gain_four, unit_four, inverse_four)
    kernel_four_grad = scale_four * conv_weight_grad(section_in, grad_four)
    section_grad = (residual_cotangent.astype(jnp.float32) + conv_transpose(grad_four, kernel_four)).astype(jnp.bfloat16)
    flat_grad = section_grad.reshape(-1, wide_channels)
    patch_grad = scale_four * lax.dot_general(patches, flat_grad, (((0,), (0,)), ((), ())), preferred_element_type=jnp.float32)
    grad_patches = lax.dot_general(flat_grad, patch_weight, (((1,), (1,)), ((), ())), preferred_element_type=jnp.float32)
    grad_merged = grad_patches.reshape(crop_count, half_height, half_breadth, 2, 2, channels)
    grad_merged = grad_merged.transpose(0, 1, 3, 2, 4, 5).reshape(crop_count, height, breadth, channels)
    merge_gain_grad = scale_three * lax.optimization_barrier(jnp.sum(grad_merged * unit_summed, axis=(0, 1, 2)))
    grad_summed = normalize_back(grad_merged * merge_gain, unit_summed, inverse_summed)
    summed_blocks = grad_summed.reshape(groups, R3 * breadth, channels)

    def backward_block(running, inputs):
        mixed_block, grad_block = inputs
        unit_mixed, inverse_mixed, normed, upward, hidden, branch = forward_block(mixed_block)
        expand_acc, project_acc, scale_acc, gain_acc = running
        scale_acc = scale_acc + lax.optimization_barrier(jnp.sum(grad_block * branch, axis=0))
        grad_branch = (layer_scale * grad_block).astype(jnp.bfloat16)
        project_acc = project_acc + lax.dot_general(hidden, grad_branch, (((0,), (0,)), ((), ())), preferred_element_type=jnp.float32)
        grad_hidden = lax.dot_general(grad_branch, project_weight, (((1,), (1,)), ((), ())), preferred_element_type=jnp.float32)
        grad_upward = (grad_hidden * gelu_slope(upward)).astype(jnp.bfloat16)
        expand_acc = expand_acc + lax.dot_general(normed, grad_upward, (((0,), (0,)), ((), ())), preferred_element_type=jnp.float32)
        grad_normed = lax.dot_general(grad_upward, expand_weight, (((1,), (1,)), ((), ())), preferred_element_type=jnp.float32)
        gain_acc = gain_acc + lax.optimization_barrier(jnp.sum(grad_normed * unit_mixed, axis=0))
        grad_mixed_block = normalize_back(grad_normed * gain_three, unit_mixed, inverse_mixed).astype(jnp.bfloat16)
        return ((expand_acc, project_acc, scale_acc, gain_acc), grad_mixed_block)
    initial = (jnp.zeros((channels, hidden_width), jnp.float32), jnp.zeros((hidden_width, channels), jnp.float32), jnp.zeros((channels,), jnp.float32), jnp.zeros((channels,), jnp.float32))
    totals, grad_blocks = lax.scan(backward_block, initial, (mixed_blocks, summed_blocks))
    grad_mixed = grad_blocks.reshape(crop_count, height, breadth, channels)
    kernel_three_grad = scale_three * conv_weight_grad(block_input, grad_mixed)
    input_grad = (grad_summed + conv_transpose(grad_mixed, kernel_three)).astype(jnp.bfloat16)
    return (input_grad, kernel_three_grad, scale_three * totals[3], scale_three * totals[0], scale_three * totals[1], scale_three * totals[2], merge_gain_grad, patch_grad, kernel_four_grad, gain_four_grad)
```

```python
import functools
import math

import jax
import jax.numpy as jnp
from jax import lax
from jax.experimental import pallas as pl
from jax.experimental.pallas import tpu as pltpu
from jax.sharding import PartitionSpec as P

EPSILON = 1e-06
F32 = jnp.float32
BF16 = jnp.bfloat16
XS, YS, ZS, KS = 4, 4, 8, 2


class Place:
    def __init__(self):
        row, col = lax.axis_index("row"), lax.axis_index("col")
        self.row, self.col = row, col
        self.x, self.z = lax.rem(row, XS), lax.div(row, XS)
        self.k, self.y = lax.rem(col, KS), lax.div(col, KS)

    def near(self, down, right):
        rows, cols = XS * ZS, YS * KS
        return {
            "row": lax.rem(self.row + (down + rows), rows),
            "col": lax.rem(self.col + (right + cols), cols),
        }

    def core_peer(self):
        return {"row": self.row, "col": self.y * KS + (1 - self.k)}

    def y_peer(self, y):
        return {"row": self.row, "col": y * KS + self.k}

    def x_peer(self, x):
        return {"row": self.z * XS + x, "col": self.col}

    def z_peer(self, z):
        return {"row": z * XS + self.x, "col": self.col}

    def col_peer(self, col):
        return {"row": self.row, "col": col}


def remote(src, dst, send, recv, device):
    return pltpu.make_async_remote_copy(
        src_ref=src,
        dst_ref=dst,
        send_sem=send,
        recv_sem=recv,
        device_id=device,
        device_id_type=pl.DeviceIdType.MESH,
    )


class Exchange:
    def __init__(self, count, me, piece, slots, send, recv, peer):
        self.others = [lax.rem(me + d, count) for d in range(1, count)]
        self.copies = [
            remote(piece(p), slots.at[me], send.at[d], recv.at[me], peer(p))
            for d, p in enumerate(self.others)
        ]
        self.arrivals = [
            remote(piece(p), slots.at[p], send.at[d], recv.at[p], peer(p))
            for d, p in enumerate(self.others)
        ]

    def start(self):
        for copy in self.copies:
            copy.start()

    def wait_recv(self):
        for copy in self.arrivals:
            copy.wait_recv()

    def wait_send(self):
        for copy in self.copies:
            copy.wait_send()


W = 16
L = W + 6
CORNERS = ((1, 1), (1, -1), (-1, 1), (-1, -1))
HALOS = ("i3", "i4", "g4", "g3")


def halo_rows(name):
    return 8 if name.endswith("3") else 4


def scratch_table():
    vm, dma = pltpu.VMEM, pltpu.SemaphoreType.DMA
    packed = lambda pixels: vm((pixels * 8, 128), F32)
    table = {
        "w1": vm((512, 2048), BF16),
        "w2": vm((2048, 512), BF16),
        "wp": vm((2048, 1024), BF16),
        "wsem": dma((3,)),
        "f3": packed(14 * L), "g3": packed(14 * L), "m3": packed(8 * W), "gs3": packed(8 * W),
        "f4": packed(10 * L), "g4": packed(10 * L), "m4": packed(4 * W),
        "k3": packed(49), "k4": packed(49), "a3": packed(49), "a4": packed(49),
        "um": vm((256, 512), F32), "im": vm((256, 128), F32), "nb": vm((256, 512), BF16),
        "hb": vm((256, 2048), BF16), "sl": vm((256, 2048), F32), "br": vm((256, 512), F32),
        "us": vm((256, 512), F32), "is": vm((256, 128), F32), "pb": vm((64, 2048), BF16),
        "fg": vm((64, 1024), BF16), "gb": vm((256, 512), BF16),
        "gu": vm((256, 2048), BF16),
    }
    for name in HALOS:
        rows = halo_rows(name)
        table["c_" + name] = vm((rows, W, 8, 128), BF16)
        table["v_" + name] = vm((2, 3, W, 8, 128), BF16)
        table["h_" + name] = vm((2, rows, 3, 8, 128), BF16)
        table["d_" + name] = vm((4, 3, 3, 8, 128), BF16)
        table["s_" + name] = dma((8,))
        table["r_" + name] = dma((8,))
    pieces = YS * XS * ZS
    for t in ("a", "b"):
        table["send_" + t] = vm((pieces, 64, 128), BF16)
        table["got_" + t] = vm((pieces, 64, 128), BF16)
        table["own_" + t] = vm((pieces, 64, 128), F32)
        table["out2_" + t] = vm((pieces, 64, 128), BF16)
        table["in2_" + t] = vm((4, 32, 64, 128), BF16)
        table["out3_" + t] = vm((32, 64, 128), BF16)
        table["in3_" + t] = vm((4, ZS, 64, 128), BF16)
        table["out4_" + t] = vm((ZS, 64, 128), BF16)
        table["in4_" + t] = vm((ZS, 64, 128), BF16)
        table["sum3_" + t] = vm((ZS, 64, 128), F32)
        for stage, count in ((2, 4), (3, 4), (4, ZS)):
            table["s%d_%s" % (stage, t)] = dma((count,))
            table["r%d_%s" % (stage, t)] = dma((count,))
    table.update(
        fin=vm((YS * KS, 128, 128), BF16),
        small=vm((192, 512), F32),
        sm_got=vm((96, 512), F32),
        sm_acc=vm((YS, 24, 512), F32),
        sm_iny=vm((YS, 24, 512), F32),
        sm_xp=vm((XS, 24, 128), F32),
        sm_inx=vm((XS, 24, 128), F32),
        sm_z=vm((ZS, 24, 128), F32),
        sm_fin=vm((XS, 24, 128), F32),
        s1=dma((3,)), r1=dma((3,)),
        sf=dma((YS * KS,)), rf=dma((YS * KS,)),
        sy=dma((YS,)), ry=dma((YS,)), sx=dma((XS,)), rx=dma((XS,)),
        sz=dma((ZS,)), rz=dma((ZS,)), sg=dma((XS,)), rg=dma((XS,)),
        sc=dma((YS * KS,)), rc=dma((YS * KS,)),
    )
    return table


def pixels_at(ref, start, count):
    return ref[pl.ds(pl.multiple_of(start * 8, 8), count * 8), :].reshape(count, 8, 128)


def put_pixels(ref, start, value):
    count = value.shape[0]
    ref[pl.ds(pl.multiple_of(start * 8, 8), count * 8), :] = value.reshape(count * 8, 128)


def taps_in(weights, ref, groups):
    lanes = 8 // groups
    for g in range(groups):
        for s in range(lanes):
            ref[pl.ds(g * lanes + s, 49, stride=8), :] = weights[:, s * 128 : (s + 1) * 128]


def quad(ref, length, row, column, g):
    dy, dx = divmod(g, 2)
    rows = []
    for yy in range(4):
        for h in range(2):
            start = ((row + 2 * yy + dy) * length + column + dx) * 8 + 4 * h
            rows.append(
                jnp.concatenate([ref[pl.ds(start + s, 8, stride=16), :] for s in range(4)], axis=1)
            )
    return jnp.concatenate(rows, axis=0)


def put_quad(ref, length, row, column, g, value):
    dy, dx = divmod(g, 2)
    for yy in range(4):
        for h in range(2):
            start = ((row + 2 * yy + dy) * length + column + dx) * 8 + 4 * h
            top = yy * 16 + h * 8
            for s in range(4):
                ref[pl.ds(start + s, 8, stride=16), :] = value[
                    top : top + 8, s * 128 : (s + 1) * 128
                ]


def flat_four(ref):
    return jnp.concatenate([ref[pl.ds(s, 64, stride=8), :] for s in range(8)], axis=1)


def put_four(ref, value):
    for i in range(4):
        for s in range(8):
            ref[pl.ds(((3 + i) * L + 3) * 8 + s, W, stride=8), :] = value[
                i * W : (i + 1) * W, s * 128 : (s + 1) * 128
            ]


def conv(framed, rows, taps, flip, out, base=None):
    def step(i, carry):
        acc = jnp.zeros((W, 8, 128), F32) if base is None else pixels_at(base, i * W, W)
        for p in range(7):
            line = pixels_at(framed, (i + p) * L, L)
            for q in range(7):
                tap = (6 - p) * 7 + 6 - q if flip else p * 7 + q
                acc = acc + line[q : q + W] * taps[tap * 8 : tap * 8 + 8, :]
        put_pixels(out, i * W, acc)
        return carry

    lax.fori_loop(0, rows, step, 0)


def tap_grads(framed, grads, rows, out):
    def over_p(p, carry):
        def over_rows(i, accs):
            line = pixels_at(framed, (i + p) * L, L)
            grad = pixels_at(grads, (i + 3) * L + 3, W)
            return tuple(acc + jnp.sum(line[q : q + W] * grad, axis=0) for q, acc in enumerate(accs))

        accs = lax.fori_loop(0, rows, over_rows, (jnp.zeros((8, 128), F32),) * 7)
        for q in range(7):
            put_pixels(out, p * 7 + q, accs[q][None])
        return carry

    lax.fori_loop(0, 7, over_p, 0)


class Halo:
    def __init__(self, at, t, name):
        self.rows = rows = halo_rows(name)
        self.at, self.t, self.name = at, t, name
        c, v, h, d = (t[key + name] for key in ("c_", "v_", "h_", "d_"))
        s, r = t["s_" + name], t["r_" + name]
        three = lambda way, size: pl.ds(size - 3, 3) if way > 0 else pl.ds(0, 3)
        self.copies = []
        for n, way in enumerate((1, -1)):
            self.copies.append(
                remote(c.at[three(way, rows)], v.at[n], s.at[n], r.at[n], at.near(way, 0))
            )
            self.copies.append(
                remote(c.at[:, three(way, W)], h.at[n], s.at[2 + n], r.at[2 + n], at.near(0, way))
            )
        for n, (down, right) in enumerate(CORNERS):
            self.copies.append(
                remote(
                    c.at[three(down, rows), three(right, W)], d.at[n], s.at[4 + n], r.at[4 + n],
                    at.near(down, right),
                )
            )

    def start(self, framed):
        c = self.t["c_" + self.name]

        def step(i, carry):
            c[i] = pixels_at(framed, (i + 3) * L + 3, W).astype(BF16)
            return carry

        lax.fori_loop(0, self.rows, step, 0)
        for copy in self.copies:
            copy.start()

    def wait_send(self):
        for copy in self.copies:
            copy.wait_send()

    def finish(self, framed):
        for copy in self.copies:
            copy.wait_recv()
        at, rows = self.at, self.rows
        v, h, d = (self.t[key + self.name] for key in ("v_", "h_", "d_"))
        one = lambda ok: jnp.where(ok, 1.0, 0.0).astype(F32)
        up, down = one(at.row > 0), one(at.row < XS * ZS - 1)
        left, right = one(at.col > 0), one(at.col < YS * KS - 1)
        for n, (ok, first) in enumerate(((up, 0), (down, rows + 3))):
            for i in range(3):
                put_pixels(framed, (first + i) * L + 3, v[n, i].astype(F32) * ok)
        for n, (side, start) in enumerate(((left, 0), (right, W + 3))):
            for i in range(rows + 6):
                if i < 3:
                    value = d[n, i].astype(F32) * (side * up)
                elif i < rows + 3:
                    value = h[n, i - 3].astype(F32) * side
                else:
                    value = d[2 + n, i - rows - 3].astype(F32) * (side * down)
                if rows == 8:
                    inner = pixels_at(framed, i * L + (W if n == 0 else 3), 3)
                    first, second = (value, inner) if n == 0 else (inner, value)
                    value = jnp.concatenate([first[:, 4:8], second[:, 0:4]], axis=1)
                put_pixels(framed, i * L + start, value)


def unit_of(values):
    mean_value = jnp.mean(values, axis=-1, keepdims=True)
    square = jnp.mean(values * values, axis=-1, keepdims=True)
    inverse = lax.rsqrt(square - mean_value * mean_value + EPSILON)
    return (values - mean_value) * inverse, inverse


def unit_back(grads, unit_values, inverse):
    return (
        grads
        - jnp.mean(grads, axis=-1, keepdims=True)
        - unit_values * jnp.mean(grads * unit_values, axis=-1, keepdims=True)
    ) * inverse


def by_rows(left, right):
    return lax.dot_general(left, right, (((0,), (0,)), ((), ())), preferred_element_type=F32)


def by_lanes(left, right):
    return lax.dot_general(left, right, (((1,), (1,)), ((), ())), preferred_element_type=F32)


def kernel(
    scale_three, scale_four, names,
    xin, k3_in, gain_three, w1_in, w2_in, layer_scale, merge_gain, wp_in, k4_in, gain_four, cot, res,
    input_o, patch_o, project_o, expand_o, small_o,
    *scratch,
):
    t = dict(zip(names, scratch))
    at = Place()
    x, y, z, k, col = at.x, at.y, at.z, at.k, at.col
    weights = [
        pltpu.make_async_copy(src, t[dst], t["wsem"].at[i])
        for i, (src, dst) in enumerate(((w1_in, "w1"), (w2_in, "w2"), (wp_in, "wp")))
    ]
    for copy in weights:
        copy.start()
    barrier = pltpu.get_barrier_semaphore()
    greeted = [at.col_peer(lax.rem(col + d, YS * KS)) for d in range(1, YS * KS)]
    greeted += [at.x_peer(lax.rem(x + d, XS)) for d in range(1, XS)]
    greeted += [at.z_peer(lax.rem(z + d, ZS)) for d in range(1, ZS)]
    greeted += [at.near(*way) for way in CORNERS + ((1, 0), (-1, 0))]
    for device in greeted:
        pl.semaphore_signal(barrier, inc=1, device_id=device, device_id_type=pl.DeviceIdType.MESH)

    f3, m3 = t["f3"], t["m3"]
    for i in range(8):
        line = xin[i].astype(F32)
        for h in range(2):
            for s in range(4):
                f3[pl.ds(((3 + i) * L + 3) * 8 + 4 * h + s, W, stride=8), :] = line[
                    h * W : (h + 1) * W, s * 128 : (s + 1) * 128
                ]
    pl.semaphore_wait(barrier, len(greeted))
    halo_i3 = Halo(at, t, "i3")
    halo_i3.start(f3)
    taps_in(k3_in, t["k3"], 2)
    taps_in(k4_in, t["k4"], 1)
    halo_i3.finish(f3)
    conv(f3, 8, t["k3"], False, m3)
    for g in range(4):
        unit, inverse = unit_of(quad(m3, W, 0, 0, g))
        part = slice(g * 64, g * 64 + 64)
        t["um"][part, :] = unit
        t["im"][part, :] = jnp.broadcast_to(inverse, (64, 128))
        t["nb"][part, :] = (unit * gain_three[...]).astype(BF16)
    weights[0].wait()

    def expand(n, carry):
        lanes = pl.ds(pl.multiple_of(n * 256, 256), 256)
        upward = jnp.dot(t["nb"][...], t["w1"][:, lanes], preferred_element_type=F32)
        cumulative = 0.5 * (1.0 + lax.erf(upward * (1.0 / math.sqrt(2.0))))
        t["hb"][:, lanes] = (upward * cumulative).astype(BF16)
        t["sl"][:, lanes] = cumulative + upward * jnp.exp(-0.5 * upward * upward) * (
            1.0 / math.sqrt(2.0 * math.pi)
        )
        return carry

    lax.fori_loop(0, 8, expand, 0)
    weights[1].wait()
    t["br"][...] = jnp.dot(t["hb"][...], t["w2"][...], preferred_element_type=F32)
    for g in range(4):
        part = slice(g * 64, g * 64 + 64)
        summed = quad(f3, L, 3, 3, g) + layer_scale[...] * t["br"][part, :]
        unit, inverse = unit_of(summed)
        t["us"][part, :] = unit
        t["is"][part, :] = jnp.broadcast_to(inverse, (64, 128))
        t["pb"][:, g * 512 : (g + 1) * 512] = (unit * merge_gain[...]).astype(BF16)
    weights[2].wait()

    f4, g4, m4 = t["f4"], t["g4"], t["m4"]
    section_in = jnp.dot(t["pb"][...], t["wp"][...], preferred_element_type=F32)
    put_four(f4, section_in.astype(BF16).astype(F32))
    halo_i4 = Halo(at, t, "i4")
    halo_i4.start(f4)
    t["small"][...] = jnp.zeros((192, 512), F32)
    halo_i4.finish(f4)
    conv(f4, 4, t["k4"], False, m4)
    unit_four, inverse_four = unit_of(flat_four(m4))
    cot_four = cot[...].astype(F32)
    gain_four_part = jnp.sum(cot_four * unit_four, axis=0, keepdims=True) * scale_four
    t["small"][171:172, :] = gain_four_part[:, 0:512]
    t["small"][172:173, :] = gain_four_part[:, 512:1024]
    put_four(g4, unit_back(cot_four * gain_four[...], unit_four, inverse_four))
    halo_g4 = Halo(at, t, "g4")
    halo_g4.start(g4)
    tap_grads(f4, g4, 4, t["a4"])
    halo_g4.finish(g4)
    conv(g4, 4, t["k4"], True, m4)
    t["fg"][...] = (res[...].astype(F32) + flat_four(m4)).astype(BF16)

    first = k == 0

    def split(index, row, even, odd, tag):
        here = slice(row, row + even.shape[0])
        t["send_" + tag][index, here, :] = jnp.where(first, odd, even).astype(BF16)
        t["own_" + tag][index, here, :] = jnp.where(first, even, odd)

    def products_a(zz, carry):
        lanes = pl.ds(pl.multiple_of(zz * 256, 256), 256)
        out = by_rows(t["pb"][:, lanes], t["fg"][...])
        for q in range(YS):
            for xx in range(XS):
                block = out[xx * 64 : (xx + 1) * 64, q * 256 : (q + 1) * 256]
                split(q * (XS * ZS) + xx * ZS + zz, 0, block[:, :128], block[:, 128:], "a")
        return carry

    lax.fori_loop(0, ZS, products_a, 0)
    core_a = remote(t["send_a"], t["got_a"], t["s1"].at[1], t["r1"].at[1], at.core_peer())
    core_a.start()

    merge_part = scale_part = jnp.zeros((1, 512), F32)
    for g in range(4):
        part = slice(g * 64, g * 64 + 64)
        unit = t["us"][part, :]
        grad_merged = by_lanes(t["fg"][...], t["wp"][g * 512 : (g + 1) * 512, :])
        merge_part = merge_part + jnp.sum(grad_merged * unit, axis=0, keepdims=True)
        grad = unit_back(grad_merged * merge_gain[...], unit, t["is"][part, 0:1])
        scale_part = scale_part + jnp.sum(grad * t["br"][part, :], axis=0, keepdims=True)
        put_quad(t["gs3"], W, 0, 0, g, grad)
        t["gb"][part, :] = (layer_scale[...] * grad).astype(BF16)
    t["small"][169:170, :] = scale_part * scale_three
    t["small"][170:171, :] = merge_part * scale_three

    def narrow(n, carry):
        lanes = pl.ds(pl.multiple_of(n * 256, 256), 256)
        grad_hidden = by_lanes(t["gb"][...], t["w2"][lanes, :])
        t["gu"][:, lanes] = (grad_hidden * t["sl"][:, lanes]).astype(BF16)
        return carry

    lax.fori_loop(0, 8, narrow, 0)

    per2 = 32

    def second(tag, me, peer):
        exchange = Exchange(
            4, me, lambda p: t["out2_" + tag].at[pl.ds(p * per2, per2)], t["in2_" + tag],
            t["s2_" + tag], t["r2_" + tag], peer,
        )
        own, got, out = t["own_" + tag], t["got_" + tag], t["out2_" + tag]
        for d, p in enumerate(exchange.others):

            def step(i, carry, p=p):
                j = p * per2 + i
                out[j] = (own[j] + got[j].astype(F32)).astype(BF16)
                return carry

            lax.fori_loop(0, per2, step, 0, unroll=4)
            exchange.copies[d].start()
        return exchange

    core_a.wait_recv()
    second_a = second("a", y, at.y_peer)

    grad_normed = by_lanes(t["gu"][...], t["w1"][...])
    gain_part = jnp.zeros((1, 512), F32)
    g3 = t["g3"]
    for g in range(4):
        part = slice(g * 64, g * 64 + 64)
        unit, grad = t["um"][part, :], grad_normed[part, :]
        gain_part = gain_part + jnp.sum(grad * unit, axis=0, keepdims=True)
        grad = unit_back(grad * gain_three[...], unit, t["im"][part, 0:1])
        put_quad(g3, L, 3, 3, g, grad.astype(BF16).astype(F32))
    t["small"][168:169, :] = gain_part * scale_three
    halo_g3 = Halo(at, t, "g3")
    halo_g3.start(g3)

    def products_b(zz, carry):
        lanes = pl.ds(pl.multiple_of(zz * 256, 256), 256)
        out = by_rows(t["hb"][:, lanes], t["gb"][...])
        for q in range(YS):
            for xx in range(XS):
                block = out[xx * 64 : (xx + 1) * 64, q * 128 : (q + 1) * 128]
                split(xx * (YS * ZS) + q * ZS + zz, 0, block[:32], block[32:], "b")
        return carry

    lax.fori_loop(0, ZS, products_b, 0)

    def products_e(pair, carry):
        lanes = pl.ds(pl.multiple_of(pair * 128, 128), 128)
        for q in range(YS):
            out = by_rows(t["nb"][:, lanes], t["gu"][:, q * 512 : (q + 1) * 512])
            for hz in range(2):
                for xx in range(XS):
                    rows = slice(hz * 64 + xx * 16, hz * 64 + xx * 16 + 16)
                    for half in range(2):
                        lane = half * 128
                        split(
                            xx * (YS * ZS) + q * ZS + 2 * pair + hz, 32 + 16 * half,
                            out[rows, lane : lane + 128], out[rows, 256 + lane : 384 + lane], "b",
                        )
        return carry

    lax.fori_loop(0, ZS // 2, products_e, 0)
    core_b = remote(t["send_b"], t["got_b"], t["s1"].at[2], t["r1"].at[2], at.core_peer())
    core_b.start()

    small = t["small"]
    tap_grads(f3, g3, 8, t["a3"])
    for s in range(4):
        lanes = slice(s * 128, (s + 1) * 128)
        small[0:49, lanes] = (
            t["a3"][pl.ds(s, 49, stride=8), :] + t["a3"][pl.ds(4 + s, 49, stride=8), :]
        ) * scale_three
        small[56:105, lanes] = t["a4"][pl.ds(s, 49, stride=8), :] * scale_four
        small[112:161, lanes] = t["a4"][pl.ds(4 + s, 49, stride=8), :] * scale_four
    half_rows = lambda which: pl.ds(pl.multiple_of(which * 96, 96), 96)
    core_s = remote(
        small.at[half_rows(1 - k)], t["sm_got"], t["s1"].at[0], t["r1"].at[0], at.core_peer()
    )
    core_s.start()
    core_b.wait_recv()
    second_b = second("b", x, at.x_peer)

    sm_acc = t["sm_acc"]
    core_s.wait_recv()
    for q in range(YS):
        mine = pl.ds(pl.multiple_of(k * 96 + q * 24, 8), 24)
        sm_acc[q] = small[mine, :] + t["sm_got"][q * 24 : (q + 1) * 24, :]
    small_y = Exchange(YS, y, lambda p: sm_acc.at[p], t["sm_iny"], t["sy"], t["ry"], at.y_peer)
    small_y.start()

    halo_g3.finish(g3)
    conv(g3, 8, t["k3"], True, m3, t["gs3"])

    def leave(i, carry):
        for h in range(2):
            row = jnp.concatenate(
                [m3[pl.ds(i * (W * 8) + 4 * h + s, W, stride=8), :] for s in range(4)], axis=1
            )
            input_o[i, h * W : (h + 1) * W, :] = row.astype(BF16)
        return carry

    lax.fori_loop(0, 8, leave, 0)

    small_y.wait_recv()
    total = sm_acc[y]
    for p in small_y.others:
        total = total + t["sm_iny"][p]
    for xx in range(XS):
        t["sm_xp"][xx] = total[:, xx * 128 : (xx + 1) * 128]
    small_x = Exchange(
        XS, x, lambda p: t["sm_xp"].at[p], t["sm_inx"], t["sx"], t["rx"], at.x_peer
    )
    small_x.start()

    def third(before, tag, me, me3, peer):
        before.wait_recv()
        own, got, slots = t["own_" + tag], t["got_" + tag], t["in2_" + tag]
        out, kept = t["out3_" + tag], t["sum3_" + tag]
        exchange = Exchange(
            4, me3, lambda p: out.at[pl.ds(p * ZS, ZS)], t["in3_" + tag],
            t["s3_" + tag], t["r3_" + tag], peer,
        )

        def total_of(i):
            j = me * per2 + i
            acc = own[j] + got[j].astype(F32)
            for p in before.others:
                acc = acc + slots[p, i].astype(F32)
            return acc

        for d, p in enumerate(exchange.others):

            def step(i, carry, p=p):
                j = p * ZS + i
                out[j] = total_of(j).astype(BF16)
                return carry

            lax.fori_loop(0, ZS, step, 0)
            exchange.copies[d].start()

        def keep(i, carry):
            kept[i] = total_of(me3 * ZS + i)
            return carry

        lax.fori_loop(0, ZS, keep, 0)
        return exchange

    third_a = third(second_a, "a", y, x, at.x_peer)

    small_x.wait_recv()
    total = t["sm_xp"][x]
    for p in small_x.others:
        total = total + t["sm_inx"][p]
    sm_z = t["sm_z"]
    sm_z[z] = total
    small_z = Exchange(ZS, z, lambda p: sm_z.at[z], sm_z, t["sz"], t["rz"], at.z_peer)
    small_z.start()

    third_b = third(second_b, "b", x, y, at.y_peer)

    def fourth(before, tag):
        before.wait_recv()
        slots, kept, out = t["in3_" + tag], t["sum3_" + tag], t["out4_" + tag]
        exchange = Exchange(
            ZS, z, lambda p: out.at[p], t["in4_" + tag], t["s4_" + tag], t["r4_" + tag], at.z_peer
        )

        def step(i, carry):
            acc = kept[i]
            for p in before.others:
                acc = acc + slots[p, i].astype(F32)
            kept[i] = acc
            out[i] = acc.astype(BF16)
            return carry

        lax.fori_loop(0, ZS, step, 0)
        exchange.start()
        return exchange

    fourth_a = fourth(third_a, "a")

    small_z.wait_recv()
    total = sm_z[0]
    for p in range(1, ZS):
        total = total + sm_z[p]
    sm_fin = t["sm_fin"]
    sm_fin[x] = total
    small_gx = Exchange(XS, x, lambda p: sm_fin.at[x], sm_fin, t["sg"], t["rg"], at.x_peer)
    small_gx.start()

    fourth_b = fourth(third_b, "b")

    small_gx.wait_recv()
    mine = k * YS + y
    small_o[mine] = jnp.concatenate([sm_fin[q] for q in range(XS)], axis=1)
    cols = [lax.rem(col + d, YS * KS) for d in range(1, YS * KS)]
    last = [
        remote(small_o.at[mine], small_o.at[mine], t["sc"].at[d], t["rc"].at[mine], at.col_peer(c))
        for d, c in enumerate(cols)
    ]
    for copy in last:
        copy.start()

    fin = t["fin"]
    for base, exchange, tag in ((0, fourth_a, "a"), (64, fourth_b, "b")):
        exchange.wait_recv()
        acc = t["sum3_" + tag][z]
        for p in exchange.others:
            acc = acc + t["in4_" + tag][p].astype(F32)
        fin[col, base : base + 64] = acc.astype(BF16)
    gather = Exchange(YS * KS, col, lambda p: fin.at[col], fin, t["sf"], t["rf"], at.col_peer)
    gather.start()

    for d, c in enumerate(cols):
        s = lax.rem(c, KS) * YS + lax.div(c, KS)
        remote(
            small_o.at[mine], small_o.at[s], t["sc"].at[d], t["rc"].at[s], at.col_peer(c)
        ).wait_recv()

    gather.wait_recv()
    for c in range(YS * KS):
        q, kk = divmod(c, KS)
        patch_o[:, c * 128 : (c + 1) * 128] = fin[c, 0:64].astype(F32) * scale_four
        project_o[kk * 32 : (kk + 1) * 32, q * 128 : (q + 1) * 128] = (
            fin[c, 64:96].astype(F32) * scale_three
        )
        for half in range(2):
            lane = c * 256 + half * 128
            expand_o[:, lane : lane + 128] = (
                fin[c, 96 + half * 16 : 112 + half * 16].astype(F32) * scale_three
            )

    for copy in (core_s, core_a, core_b):
        copy.wait_send()
    for exchange in (
        halo_i3, halo_i4, halo_g4, halo_g3,
        second_a, second_b, third_a, third_b, fourth_a, fourth_b, gather,
        small_y, small_x, small_z, small_gx,
    ):
        exchange.wait_send()
    for copy in last:
        copy.wait_send()


def body(
    block_input,
    kernel_three,
    gain_three,
    expand_weight,
    project_weight,
    layer_scale,
    merge_gain,
    patch_weight,
    kernel_four,
    gain_four,
    normed_cotangent,
    residual_cotangent,
):
    devices = lax.axis_size("row") * lax.axis_size("col")
    scale_three = 1.0 / math.sqrt(256 * devices)
    scale_four = 1.0 / math.sqrt(64 * devices)
    table = scratch_table()
    whole = pl.BlockSpec(memory_space=pltpu.VMEM)
    away = pl.BlockSpec(memory_space=pl.ANY)
    ins = [whole] * 12
    for place in (3, 4, 7):
        ins[place] = away
    flat = lambda v: v.reshape(1, -1)
    input_grad, patch_grad, project_grad, expand_grad, small = pl.pallas_call(
        functools.partial(kernel, scale_three, scale_four, tuple(table)),
        out_shape=(
            jax.ShapeDtypeStruct((8, 32, 512), BF16),
            jax.ShapeDtypeStruct((64, 1024), F32),
            jax.ShapeDtypeStruct((64, 512), F32),
            jax.ShapeDtypeStruct((16, 2048), F32),
            jax.ShapeDtypeStruct((8, 24, 512), F32),
        ),
        in_specs=ins,
        out_specs=(whole,) * 5,
        scratch_shapes=list(table.values()),
        compiler_params=pltpu.CompilerParams(
            collective_id=0, has_side_effects=True, vmem_limit_bytes=60 << 20
        ),
        name="block_backward",
    )(
        block_input.reshape(8, 32, 512),
        kernel_three.reshape(49, 512),
        flat(gain_three),
        expand_weight,
        project_weight,
        flat(layer_scale),
        flat(merge_gain),
        patch_weight,
        kernel_four.reshape(49, 1024),
        flat(gain_four),
        normed_cotangent.reshape(64, 1024),
        residual_cotangent.reshape(64, 1024),
    )
    small = small.reshape(192, 512)
    return (
        input_grad.reshape(1, 8, 32, 512),
        small[0:49].reshape(7, 7, 512),
        small[168],
        expand_grad,
        project_grad,
        small[169],
        small[170],
        patch_grad,
        jnp.concatenate([small[56:105], small[112:161]], axis=1).reshape(7, 7, 1024),
        small[171:173].reshape(-1),
    )


def solution(mesh):
    pixels = P(None, "row", "col", None)
    return jax.shard_map(
        body,
        mesh=mesh,
        in_specs=(pixels,) + (P(),) * 9 + (pixels, pixels),
        out_specs=(pixels, P(), P(), P("row", None), P("row", None), P(), P(), P("row", None), P(), P()),
        check_vma=False,
    )
```

```python
import functools
import math

import jax
import jax.numpy as jnp
from jax import lax
from jax.experimental import pallas as pl
from jax.experimental.pallas import tpu as pltpu
from jax.sharding import PartitionSpec as P

EPSILON = 1e-06
F32 = jnp.float32
BF16 = jnp.bfloat16
XS, YS, ZS, KS = 4, 4, 8, 2


class Place:
    def __init__(self):
        row, col = lax.axis_index("row"), lax.axis_index("col")
        self.row, self.col = row, col
        self.x, self.z = lax.rem(row, XS), lax.div(row, XS)
        self.k, self.y = lax.rem(col, KS), lax.div(col, KS)

    def near(self, down, right):
        rows, cols = XS * ZS, YS * KS
        return {
            "row": lax.rem(self.row + (down + rows), rows),
            "col": lax.rem(self.col + (right + cols), cols),
        }

    def core_peer(self):
        return {"row": self.row, "col": self.y * KS + (1 - self.k)}

    def y_peer(self, y):
        return {"row": self.row, "col": y * KS + self.k}

    def x_peer(self, x):
        return {"row": self.z * XS + x, "col": self.col}

    def z_peer(self, z):
        return {"row": z * XS + self.x, "col": self.col}

    def col_peer(self, col):
        return {"row": self.row, "col": col}


def remote(src, dst, send, recv, device):
    return pltpu.make_async_remote_copy(
        src_ref=src,
        dst_ref=dst,
        send_sem=send,
        recv_sem=recv,
        device_id=device,
        device_id_type=pl.DeviceIdType.MESH,
    )


class Exchange:
    def __init__(self, count, me, piece, slots, send, recv, peer):
        self.others = [lax.rem(me + d, count) for d in range(1, count)]
        self.copies = [
            remote(piece(p), slots.at[me], send.at[d], recv.at[me], peer(p))
            for d, p in enumerate(self.others)
        ]
        self.arrivals = [
            remote(piece(p), slots.at[p], send.at[d], recv.at[p], peer(p))
            for d, p in enumerate(self.others)
        ]

    def start(self):
        for copy in self.copies:
            copy.start()

    def wait_recv(self):
        for copy in self.arrivals:
            copy.wait_recv()

    def wait_send(self):
        for copy in self.copies:
            copy.wait_send()


W = 16
L = W + 6
CORNERS = ((1, 1), (1, -1), (-1, 1), (-1, -1))
HALOS = ("i3", "i4", "g4", "g3")
CHAINS = ("a1", "a2", "b1", "b2")
Y_FIRST = ("a1", "b2")


def halo_rows(name):
    return 8 if name.endswith("3") else 4


def scratch_table():
    vm, dma = pltpu.VMEM, pltpu.SemaphoreType.DMA
    packed = lambda pixels: vm((pixels * 8, 128), F32)
    table = {
        "w1": vm((512, 2048), BF16),
        "w2": vm((2048, 512), BF16),
        "wp": vm((2048, 1024), BF16),
        "wsem": dma((3,)),
        "f3": packed(14 * L), "g3": packed(14 * L), "m3": packed(8 * W), "gs3": packed(8 * W),
        "f4": packed(10 * L), "g4": packed(10 * L), "m4": packed(4 * W),
        "k3": packed(49), "k4": packed(49), "a3": packed(49), "a4": packed(49),
        "um": vm((256, 512), F32), "im": vm((256, 128), F32), "nb": vm((256, 512), BF16),
        "hb": vm((256, 2048), BF16), "sl": vm((256, 2048), F32), "br": vm((256, 512), F32),
        "us": vm((256, 512), F32), "is": vm((256, 128), F32), "pb": vm((64, 2048), BF16),
        "fg": vm((64, 1024), BF16), "gb": vm((256, 512), BF16),
        "gu": vm((256, 2048), BF16),
    }
    for name in HALOS:
        rows = halo_rows(name)
        table["c_" + name] = vm((rows, W, 8, 128), BF16)
        table["v_" + name] = vm((2, 3, W, 8, 128), BF16)
        table["h_" + name] = vm((2, rows, 3, 8, 128), BF16)
        table["d_" + name] = vm((4, 3, 3, 8, 128), BF16)
        table["s_" + name] = dma((8,))
        table["r_" + name] = dma((8,))
    pieces = YS * XS * ZS
    for t in CHAINS:
        table["send_" + t] = vm((pieces, 32, 128), BF16)
        table["got_" + t] = vm((pieces, 32, 128), BF16)
        table["own_" + t] = vm((pieces, 32, 128), F32)
        table["out2_" + t] = vm((pieces, 32, 128), BF16)
        table["in2_" + t] = vm((4, 32, 32, 128), BF16)
        table["out3_" + t] = vm((32, 32, 128), BF16)
        table["in3_" + t] = vm((4, ZS, 32, 128), BF16)
        table["out4_" + t] = vm((ZS, 32, 128), BF16)
        table["in4_" + t] = vm((ZS, 32, 128), BF16)
        table["sum3_" + t] = vm((ZS, 32, 128), F32)
        for stage, count in ((2, 4), (3, 4), (4, ZS)):
            table["s%d_%s" % (stage, t)] = dma((count,))
            table["r%d_%s" % (stage, t)] = dma((count,))
    table.update(
        xin=vm((8, 32, 512), BF16), kin3=vm((7, 7, 512), F32), kin4=vm((7, 7, 1024), F32),
        gain3=vm((1, 512), F32), scale=vm((1, 512), F32), mgain=vm((1, 512), F32),
        gain4=vm((1, 1024), F32), cot=vm((64, 1024), BF16), res=vm((64, 1024), BF16),
        isem=dma((9,)), osem=dma((1,)), xout=vm((8, 32, 512), BF16),
        small=vm((192, 512), F32),
        sm_got=vm((96, 512), F32),
        sm_acc=vm((YS, 24, 512), F32),
        sm_iny=vm((YS, 24, 512), F32),
        sm_xp=vm((XS, 24, 128), F32),
        sm_inx=vm((XS, 24, 128), F32),
        sm_z=vm((ZS, 24, 128), F32),
        sm_fin=vm((XS, 24, 128), F32),
        s1=dma((5,)), r1=dma((5,)),
        sfa=dma((YS * KS,)), rfa=dma((YS * KS,)), sfb=dma((YS * KS,)), rfb=dma((YS * KS,)),
        sy=dma((YS,)), ry=dma((YS,)), sx=dma((XS,)), rx=dma((XS,)),
        sz=dma((ZS,)), rz=dma((ZS,)), sg=dma((XS,)), rg=dma((XS,)),
        sc=dma((YS * KS,)), rc=dma((YS * KS,)),
    )
    return table


def pixels_at(ref, start, count):
    return ref[pl.ds(pl.multiple_of(start * 8, 8), count * 8), :].reshape(count, 8, 128)


def put_pixels(ref, start, value):
    count = value.shape[0]
    ref[pl.ds(pl.multiple_of(start * 8, 8), count * 8), :] = value.reshape(count * 8, 128)


def taps_in(weights, ref, groups):
    lanes = 8 // groups
    for p in range(7):
        line = weights[p]
        for g in range(groups):
            for s in range(lanes):
                ref[pl.ds(p * 56 + g * lanes + s, 7, stride=8), :] = line[
                    :, s * 128 : (s + 1) * 128
                ]


def quad(ref, length, row, column, g):
    dy, dx = divmod(g, 2)
    rows = []
    for yy in range(4):
        for h in range(2):
            start = ((row + 2 * yy + dy) * length + column + dx) * 8 + 4 * h
            rows.append(
                jnp.concatenate([ref[pl.ds(start + s, 8, stride=16), :] for s in range(4)], axis=1)
            )
    return jnp.concatenate(rows, axis=0)


def put_quad(ref, length, row, column, g, value):
    dy, dx = divmod(g, 2)
    for yy in range(4):
        for h in range(2):
            start = ((row + 2 * yy + dy) * length + column + dx) * 8 + 4 * h
            top = yy * 16 + h * 8
            for s in range(4):
                ref[pl.ds(start + s, 8, stride=16), :] = value[
                    top : top + 8, s * 128 : (s + 1) * 128
                ]


def flat_four(ref):
    return jnp.concatenate([ref[pl.ds(s, 64, stride=8), :] for s in range(8)], axis=1)


def put_four(ref, value):
    for i in range(4):
        for s in range(8):
            ref[pl.ds(((3 + i) * L + 3) * 8 + s, W, stride=8), :] = value[
                i * W : (i + 1) * W, s * 128 : (s + 1) * 128
            ]


def conv(framed, rows, taps, flip, out, base=None):
    def step(i, carry):
        acc = jnp.zeros((W, 8, 128), F32) if base is None else pixels_at(base, i * W, W)
        for p in range(7):
            line = pixels_at(framed, (i + p) * L, L)
            for q in range(7):
                tap = (6 - p) * 7 + 6 - q if flip else p * 7 + q
                acc = acc + line[q : q + W] * taps[tap * 8 : tap * 8 + 8, :]
        put_pixels(out, i * W, acc)
        return carry

    lax.fori_loop(0, rows, step, 0)


def tap_grads(framed, grads, rows, out):
    def over_p(p, carry):
        def over_rows(i, accs):
            line = pixels_at(framed, (i + p) * L, L)
            grad = pixels_at(grads, (i + 3) * L + 3, W)
            return tuple(acc + jnp.sum(line[q : q + W] * grad, axis=0) for q, acc in enumerate(accs))

        accs = lax.fori_loop(0, rows, over_rows, (jnp.zeros((8, 128), F32),) * 7)
        for q in range(7):
            put_pixels(out, p * 7 + q, accs[q][None])
        return carry

    lax.fori_loop(0, 7, over_p, 0)


class Halo:
    def __init__(self, at, t, name):
        self.rows = rows = halo_rows(name)
        self.at, self.t, self.name = at, t, name
        c, v, h, d = (t[key + name] for key in ("c_", "v_", "h_", "d_"))
        s, r = t["s_" + name], t["r_" + name]
        three = lambda way, size: pl.ds(size - 3, 3) if way > 0 else pl.ds(0, 3)
        self.copies = []
        for n, way in enumerate((1, -1)):
            self.copies.append(
                remote(c.at[three(way, rows)], v.at[n], s.at[n], r.at[n], at.near(way, 0))
            )
            self.copies.append(
                remote(c.at[:, three(way, W)], h.at[n], s.at[2 + n], r.at[2 + n], at.near(0, way))
            )
        for n, (down, right) in enumerate(CORNERS):
            self.copies.append(
                remote(
                    c.at[three(down, rows), three(right, W)], d.at[n], s.at[4 + n], r.at[4 + n],
                    at.near(down, right),
                )
            )

    def start(self, framed):
        c = self.t["c_" + self.name]

        def step(i, carry):
            c[i] = pixels_at(framed, (i + 3) * L + 3, W).astype(BF16)
            return carry

        lax.fori_loop(0, self.rows, step, 0)
        for copy in self.copies:
            copy.start()

    def wait_send(self):
        for copy in self.copies:
            copy.wait_send()

    def finish(self, framed):
        for copy in self.copies:
            copy.wait_recv()
        at, rows = self.at, self.rows
        v, h, d = (self.t[key + self.name] for key in ("v_", "h_", "d_"))
        one = lambda ok: jnp.where(ok, 1.0, 0.0).astype(F32)
        up, down = one(at.row > 0), one(at.row < XS * ZS - 1)
        left, right = one(at.col > 0), one(at.col < YS * KS - 1)
        for n, (ok, first) in enumerate(((up, 0), (down, rows + 3))):
            for i in range(3):
                put_pixels(framed, (first + i) * L + 3, v[n, i].astype(F32) * ok)
        for n, (side, start) in enumerate(((left, 0), (right, W + 3))):
            for i in range(rows + 6):
                if i < 3:
                    value = d[n, i].astype(F32) * (side * up)
                elif i < rows + 3:
                    value = h[n, i - 3].astype(F32) * side
                else:
                    value = d[2 + n, i - rows - 3].astype(F32) * (side * down)
                if rows == 8:
                    inner = pixels_at(framed, i * L + (W if n == 0 else 3), 3)
                    first, second = (value, inner) if n == 0 else (inner, value)
                    value = jnp.concatenate([first[:, 4:8], second[:, 0:4]], axis=1)
                put_pixels(framed, i * L + start, value)


def unit_of(values):
    mean_value = jnp.mean(values, axis=-1, keepdims=True)
    square = jnp.mean(values * values, axis=-1, keepdims=True)
    inverse = lax.rsqrt(square - mean_value * mean_value + EPSILON)
    return (values - mean_value) * inverse, inverse


def unit_back(grads, unit_values, inverse):
    return (
        grads
        - jnp.mean(grads, axis=-1, keepdims=True)
        - unit_values * jnp.mean(grads * unit_values, axis=-1, keepdims=True)
    ) * inverse


def by_rows(left, right):
    return lax.dot_general(left, right, (((0,), (0,)), ((), ())), preferred_element_type=F32)


def by_lanes(left, right):
    return lax.dot_general(left, right, (((1,), (1,)), ((), ())), preferred_element_type=F32)


def kernel(
    scale_three, scale_four, names,
    x_in, k3_in, gain3_in, w1_in, w2_in, scale_in, mgain_in, wp_in, k4_in, gain4_in, cot_in, res_in,
    input_o, fin_a, fin_b, small_o,
    *scratch,
):
    t = dict(zip(names, scratch))
    at = Place()
    x, y, z, k, col = at.x, at.y, at.z, at.k, at.col
    barrier = pltpu.get_barrier_semaphore()
    greeted = [at.col_peer(lax.rem(col + d, YS * KS)) for d in range(1, YS * KS)]
    greeted += [at.x_peer(lax.rem(x + d, XS)) for d in range(1, XS)]
    greeted += [at.z_peer(lax.rem(z + d, ZS)) for d in range(1, ZS)]
    greeted += [at.near(*way) for way in CORNERS + ((1, 0), (-1, 0))]
    for device in greeted:
        pl.semaphore_signal(barrier, inc=1, device_id=device, device_id_type=pl.DeviceIdType.MESH)
    params = [
        pltpu.make_async_copy(src, t[dst], t["isem"].at[i])
        for i, (src, dst) in enumerate(
            (
                (x_in, "xin"), (k3_in, "kin3"), (k4_in, "kin4"), (gain3_in, "gain3"),
                (scale_in, "scale"), (mgain_in, "mgain"), (gain4_in, "gain4"),
                (cot_in, "cot"), (res_in, "res"),
            )
        )
    ]
    weights = [
        pltpu.make_async_copy(src, t[dst], t["wsem"].at[i])
        for i, (src, dst) in enumerate(((w1_in, "w1"), (w2_in, "w2"), (wp_in, "wp")))
    ]
    for copy in params + weights:
        copy.start()
    for copy in params:
        copy.wait()
    xin, gain_three, layer_scale, merge_gain, gain_four, cot, res = (
        t[key] for key in ("xin", "gain3", "scale", "mgain", "gain4", "cot", "res")
    )

    f3, m3 = t["f3"], t["m3"]
    for i in range(8):
        line = xin[i].astype(F32)
        for h in range(2):
            for s in range(4):
                f3[pl.ds(((3 + i) * L + 3) * 8 + 4 * h + s, W, stride=8), :] = line[
                    h * W : (h + 1) * W, s * 128 : (s + 1) * 128
                ]
    taps_in(t["kin3"], t["k3"], 2)
    taps_in(t["kin4"], t["k4"], 1)
    pl.semaphore_wait(barrier, len(greeted))
    halo_i3 = Halo(at, t, "i3")
    halo_i3.start(f3)
    halo_i3.finish(f3)
    conv(f3, 8, t["k3"], False, m3)
    for g in range(4):
        unit, inverse = unit_of(quad(m3, W, 0, 0, g))
        part = slice(g * 64, g * 64 + 64)
        t["um"][part, :] = unit
        t["im"][part, :] = jnp.broadcast_to(inverse, (64, 128))
        t["nb"][part, :] = (unit * gain_three[...]).astype(BF16)
    weights[0].wait()

    def expand(n, carry):
        lanes = pl.ds(pl.multiple_of(n * 256, 256), 256)
        upward = jnp.dot(t["nb"][...], t["w1"][:, lanes], preferred_element_type=F32)
        cumulative = 0.5 * (1.0 + lax.erf(upward * (1.0 / math.sqrt(2.0))))
        t["hb"][:, lanes] = (upward * cumulative).astype(BF16)
        t["sl"][:, lanes] = cumulative + upward * jnp.exp(-0.5 * upward * upward) * (
            1.0 / math.sqrt(2.0 * math.pi)
        )
        return carry

    lax.fori_loop(0, 8, expand, 0)
    weights[1].wait()
    t["br"][...] = jnp.dot(t["hb"][...], t["w2"][...], preferred_element_type=F32)
    for g in range(4):
        part = slice(g * 64, g * 64 + 64)
        summed = quad(f3, L, 3, 3, g) + layer_scale[...] * t["br"][part, :]
        unit, inverse = unit_of(summed)
        t["us"][part, :] = unit
        t["is"][part, :] = jnp.broadcast_to(inverse, (64, 128))
        t["pb"][:, g * 512 : (g + 1) * 512] = (unit * merge_gain[...]).astype(BF16)
    weights[2].wait()

    f4, g4, m4 = t["f4"], t["g4"], t["m4"]
    section_in = jnp.dot(t["pb"][...], t["wp"][...], preferred_element_type=F32)
    put_four(f4, section_in.astype(BF16).astype(F32))
    halo_i4 = Halo(at, t, "i4")
    halo_i4.start(f4)
    t["small"][...] = jnp.zeros((192, 512), F32)
    halo_i4.finish(f4)
    conv(f4, 4, t["k4"], False, m4)
    unit_four, inverse_four = unit_of(flat_four(m4))
    cot_four = cot[...].astype(F32)
    gain_four_part = jnp.sum(cot_four * unit_four, axis=0, keepdims=True) * scale_four
    t["small"][171:172, :] = gain_four_part[:, 0:512]
    t["small"][172:173, :] = gain_four_part[:, 512:1024]
    put_four(g4, unit_back(cot_four * gain_four[...], unit_four, inverse_four))
    halo_g4 = Halo(at, t, "g4")
    halo_g4.start(g4)
    tap_grads(f4, g4, 4, t["a4"])
    halo_g4.finish(g4)
    conv(g4, 4, t["k4"], True, m4)
    t["fg"][...] = (res[...].astype(F32) + flat_four(m4)).astype(BF16)

    first = k == 0

    def split(index, row, even, odd, tag):
        here = slice(row, row + even.shape[0])
        t["send_" + tag][index, here, :] = jnp.where(first, odd, even).astype(BF16)
        t["own_" + tag][index, here, :] = jnp.where(first, even, odd)

    def products_a(zz, carry):
        lanes = pl.ds(pl.multiple_of(zz * 256, 256), 256)
        out = by_rows(t["pb"][:, lanes], t["fg"][...])
        for q in range(YS):
            for xx in range(XS):
                block = out[xx * 64 : (xx + 1) * 64, q * 256 : (q + 1) * 256]
                split(q * (XS * ZS) + xx * ZS + zz, 0, block[:32, :128], block[:32, 128:], "a1")
                split(xx * (YS * ZS) + q * ZS + zz, 0, block[32:, :128], block[32:, 128:], "a2")
        return carry

    lax.fori_loop(0, ZS, products_a, 0)
    core = {}

    def cross(tag):
        n = CHAINS.index(tag)
        core[tag] = remote(
            t["send_" + tag], t["got_" + tag], t["s1"].at[n], t["r1"].at[n], at.core_peer()
        )
        core[tag].start()

    cross("a1")
    cross("a2")

    merge_part = scale_part = jnp.zeros((1, 512), F32)
    for g in range(4):
        part = slice(g * 64, g * 64 + 64)
        unit = t["us"][part, :]
        grad_merged = by_lanes(t["fg"][...], t["wp"][g * 512 : (g + 1) * 512, :])
        merge_part = merge_part + jnp.sum(grad_merged * unit, axis=0, keepdims=True)
        grad = unit_back(grad_merged * merge_gain[...], unit, t["is"][part, 0:1])
        scale_part = scale_part + jnp.sum(grad * t["br"][part, :], axis=0, keepdims=True)
        put_quad(t["gs3"], W, 0, 0, g, grad)
        t["gb"][part, :] = (layer_scale[...] * grad).astype(BF16)
    t["small"][169:170, :] = scale_part * scale_three
    t["small"][170:171, :] = merge_part * scale_three

    def products_b(zz, carry):
        lanes = pl.ds(pl.multiple_of(zz * 256, 256), 256)
        out = by_rows(t["hb"][:, lanes], t["gb"][...])
        for q in range(YS):
            for xx in range(XS):
                block = out[xx * 64 : (xx + 1) * 64, q * 128 : (q + 1) * 128]
                split(xx * (YS * ZS) + q * ZS + zz, 0, block[:32], block[32:], "b1")
        return carry

    lax.fori_loop(0, ZS, products_b, 0)
    cross("b1")

    per2 = 32

    def second(tag):
        me, peer = (y, at.y_peer) if tag in Y_FIRST else (x, at.x_peer)
        core[tag].wait_recv()
        exchange = Exchange(
            4, me, lambda p: t["out2_" + tag].at[pl.ds(p * per2, per2)], t["in2_" + tag],
            t["s2_" + tag], t["r2_" + tag], peer,
        )
        own, got, out = t["own_" + tag], t["got_" + tag], t["out2_" + tag]
        for d, p in enumerate(exchange.others):

            def step(i, carry, p=p):
                j = p * per2 + i
                out[j] = (own[j] + got[j].astype(F32)).astype(BF16)
                return carry

            lax.fori_loop(0, per2, step, 0, unroll=4)
            exchange.copies[d].start()
        return exchange

    seconds = {"a1": second("a1"), "a2": second("a2")}

    def narrow(n, carry):
        lanes = pl.ds(pl.multiple_of(n * 256, 256), 256)
        grad_hidden = by_lanes(t["gb"][...], t["w2"][lanes, :])
        t["gu"][:, lanes] = (grad_hidden * t["sl"][:, lanes]).astype(BF16)
        return carry

    lax.fori_loop(0, 8, narrow, 0)

    seconds["b1"] = second("b1")

    grad_normed = by_lanes(t["gu"][...], t["w1"][...])
    gain_part = jnp.zeros((1, 512), F32)
    g3 = t["g3"]
    for g in range(4):
        part = slice(g * 64, g * 64 + 64)
        unit, grad = t["um"][part, :], grad_normed[part, :]
        gain_part = gain_part + jnp.sum(grad * unit, axis=0, keepdims=True)
        grad = unit_back(grad * gain_three[...], unit, t["im"][part, 0:1])
        put_quad(g3, L, 3, 3, g, grad.astype(BF16).astype(F32))
    t["small"][168:169, :] = gain_part * scale_three
    halo_g3 = Halo(at, t, "g3")
    halo_g3.start(g3)

    def products_e(pair, carry):
        lanes = pl.ds(pl.multiple_of(pair * 128, 128), 128)
        for q in range(YS):
            out = by_rows(t["nb"][:, lanes], t["gu"][:, q * 512 : (q + 1) * 512])
            for hz in range(2):
                for xx in range(XS):
                    rows = slice(hz * 64 + xx * 16, hz * 64 + xx * 16 + 16)
                    for half in range(2):
                        lane = half * 128
                        split(
                            q * (XS * ZS) + xx * ZS + 2 * pair + hz, 16 * half,
                            out[rows, lane : lane + 128], out[rows, 256 + lane : 384 + lane], "b2",
                        )
        return carry

    lax.fori_loop(0, ZS // 2, products_e, 0)
    cross("b2")

    small = t["small"]
    tap_grads(f3, g3, 8, t["a3"])
    for s in range(4):
        lanes = slice(s * 128, (s + 1) * 128)
        small[0:49, lanes] = (
            t["a3"][pl.ds(s, 49, stride=8), :] + t["a3"][pl.ds(4 + s, 49, stride=8), :]
        ) * scale_three
        small[56:105, lanes] = t["a4"][pl.ds(s, 49, stride=8), :] * scale_four
        small[112:161, lanes] = t["a4"][pl.ds(4 + s, 49, stride=8), :] * scale_four
    half_rows = lambda which: pl.ds(pl.multiple_of(which * 96, 96), 96)
    core_s = remote(
        small.at[half_rows(1 - k)], t["sm_got"], t["s1"].at[4], t["r1"].at[4], at.core_peer()
    )
    core_s.start()
    seconds["b2"] = second("b2")

    sm_acc = t["sm_acc"]
    core_s.wait_recv()
    for q in range(YS):
        mine = pl.ds(pl.multiple_of(k * 96 + q * 24, 8), 24)
        sm_acc[q] = small[mine, :] + t["sm_got"][q * 24 : (q + 1) * 24, :]
    small_y = Exchange(YS, y, lambda p: sm_acc.at[p], t["sm_iny"], t["sy"], t["ry"], at.y_peer)
    small_y.start()

    halo_g3.finish(g3)
    conv(g3, 8, t["k3"], True, m3, t["gs3"])

    def leave(i, carry):
        for h in range(2):
            row = jnp.concatenate(
                [m3[pl.ds(i * (W * 8) + 4 * h + s, W, stride=8), :] for s in range(4)], axis=1
            )
            t["xout"][i, h * W : (h + 1) * W, :] = row.astype(BF16)
        return carry

    lax.fori_loop(0, 8, leave, 0)
    out_copy = pltpu.make_async_copy(t["xout"], input_o, t["osem"].at[0])
    out_copy.start()

    small_y.wait_recv()
    total = sm_acc[y]
    for p in small_y.others:
        total = total + t["sm_iny"][p]
    for xx in range(XS):
        t["sm_xp"][xx] = total[:, xx * 128 : (xx + 1) * 128]
    small_x = Exchange(
        XS, x, lambda p: t["sm_xp"].at[p], t["sm_inx"], t["sx"], t["rx"], at.x_peer
    )
    small_x.start()

    def third(tag):
        before = seconds[tag]
        me, me3, peer = (y, x, at.x_peer) if tag in Y_FIRST else (x, y, at.y_peer)
        before.wait_recv()
        own, got, slots = t["own_" + tag], t["got_" + tag], t["in2_" + tag]
        out, kept = t["out3_" + tag], t["sum3_" + tag]
        exchange = Exchange(
            4, me3, lambda p: out.at[pl.ds(p * ZS, ZS)], t["in3_" + tag],
            t["s3_" + tag], t["r3_" + tag], peer,
        )

        def total_of(i):
            j = me * per2 + i
            acc = own[j] + got[j].astype(F32)
            for p in before.others:
                acc = acc + slots[p, i].astype(F32)
            return acc

        for d, p in enumerate(exchange.others):

            def step(i, carry, p=p):
                j = p * ZS + i
                out[j] = total_of(j).astype(BF16)
                return carry

            lax.fori_loop(0, ZS, step, 0)
            exchange.copies[d].start()

        def keep(i, carry):
            kept[i] = total_of(me3 * ZS + i)
            return carry

        lax.fori_loop(0, ZS, keep, 0)
        return exchange

    thirds = {"a1": third("a1"), "a2": third("a2")}

    small_x.wait_recv()
    total = t["sm_xp"][x]
    for p in small_x.others:
        total = total + t["sm_inx"][p]
    sm_z = t["sm_z"]
    sm_z[z] = total
    small_z = Exchange(ZS, z, lambda p: sm_z.at[z], sm_z, t["sz"], t["rz"], at.z_peer)
    small_z.start()

    thirds["b1"] = third("b1")
    thirds["b2"] = third("b2")

    def fourth(tag):
        before = thirds[tag]
        before.wait_recv()
        slots, kept, out = t["in3_" + tag], t["sum3_" + tag], t["out4_" + tag]
        exchange = Exchange(
            ZS, z, lambda p: out.at[p], t["in4_" + tag], t["s4_" + tag], t["r4_" + tag], at.z_peer
        )

        def step(i, carry):
            acc = kept[i]
            for p in before.others:
                acc = acc + slots[p, i].astype(F32)
            kept[i] = acc
            out[i] = acc.astype(BF16)
            return carry

        lax.fori_loop(0, ZS, step, 0)
        exchange.start()
        return exchange

    fourths = {"a1": fourth("a1"), "a2": fourth("a2")}

    small_z.wait_recv()
    total = sm_z[0]
    for p in range(1, ZS):
        total = total + sm_z[p]
    sm_fin = t["sm_fin"]
    sm_fin[x] = total
    small_gx = Exchange(XS, x, lambda p: sm_fin.at[x], sm_fin, t["sg"], t["rg"], at.x_peer)
    small_gx.start()

    fourths["b1"] = fourth("b1")
    fourths["b2"] = fourth("b2")

    small_gx.wait_recv()
    slot = lambda c: pl.ds(pl.multiple_of((lax.rem(c, KS) * YS + lax.div(c, KS)) * 24, 8), 24)
    number = lambda c: lax.rem(c, KS) * YS + lax.div(c, KS)
    mine = slot(col)
    small_o[mine, :] = jnp.concatenate([sm_fin[q] for q in range(XS)], axis=1)
    cols = [lax.rem(col + d, YS * KS) for d in range(1, YS * KS)]
    last = [
        remote(
            small_o.at[mine], small_o.at[mine], t["sc"].at[d], t["rc"].at[number(col)],
            at.col_peer(c),
        )
        for d, c in enumerate(cols)
    ]
    for copy in last:
        copy.start()

    def collect(tags, fin, send, recv):
        for base, tag in zip((0, 32), tags):
            exchange = fourths[tag]
            exchange.wait_recv()
            acc = t["sum3_" + tag][z]
            for p in exchange.others:
                acc = acc + t["in4_" + tag][p].astype(F32)
            fin[col, base : base + 32] = acc.astype(BF16)
        gather = Exchange(YS * KS, col, lambda p: fin.at[col], fin, send, recv, at.col_peer)
        gather.start()
        return gather

    gather_a = collect(("a1", "a2"), fin_a, t["sfa"], t["rfa"])
    gather_b = collect(("b1", "b2"), fin_b, t["sfb"], t["rfb"])

    for d, c in enumerate(cols):
        remote(
            small_o.at[mine], small_o.at[slot(c)], t["sc"].at[d], t["rc"].at[number(c)],
            at.col_peer(c),
        ).wait_recv()
    gather_a.wait_recv()
    gather_b.wait_recv()
    out_copy.wait()

    for copy in [core_s] + [core[tag] for tag in CHAINS]:
        copy.wait_send()
    for tag in CHAINS:
        for stage in (seconds, thirds, fourths):
            stage[tag].wait_send()
    for exchange in (
        halo_i3, halo_i4, halo_g4, halo_g3,
        gather_a, gather_b,
        small_y, small_x, small_z, small_gx,
    ):
        exchange.wait_send()
    for copy in last:
        copy.wait_send()


def results_kernel(
    scale_three, scale_four, input_i, fin_a, fin_b, small,
    input_o, k3_o, gain3_o, expand_o, project_o, scale_o, merge_o, patch_o, k4_o, gain4_o,
    sem,
):
    move = pltpu.make_async_copy(input_i, input_o, sem.at[0])
    move.start()
    for c in range(YS * KS):
        q, kk = divmod(c, KS)
        patch_o[:, c * 128 : (c + 1) * 128] = fin_a[c].astype(F32) * scale_four
        project_o[kk * 32 : (kk + 1) * 32, q * 128 : (q + 1) * 128] = (
            fin_b[c, 0:32].astype(F32) * scale_three
        )
        for half in range(2):
            lane = c * 256 + half * 128
            expand_o[:, lane : lane + 128] = (
                fin_b[c, 32 + half * 16 : 48 + half * 16].astype(F32) * scale_three
            )
    for p in range(7):
        k3_o[p] = small[7 * p : 7 * p + 7, :]
        k4_o[p, :, 0:512] = small[56 + 7 * p : 63 + 7 * p, :]
        k4_o[p, :, 512:1024] = small[112 + 7 * p : 119 + 7 * p, :]
    gain3_o[...] = small[168:169, :]
    scale_o[...] = small[169:170, :]
    merge_o[...] = small[170:171, :]
    gain4_o[:, 0:512] = small[171:172, :]
    gain4_o[:, 512:1024] = small[172:173, :]
    move.wait()


def body(
    block_input,
    kernel_three,
    gain_three,
    expand_weight,
    project_weight,
    layer_scale,
    merge_gain,
    patch_weight,
    kernel_four,
    gain_four,
    normed_cotangent,
    residual_cotangent,
):
    devices = lax.axis_size("row") * lax.axis_size("col")
    scale_three = 1.0 / math.sqrt(256 * devices)
    scale_four = 1.0 / math.sqrt(64 * devices)
    table = scratch_table()
    whole = pl.BlockSpec(memory_space=pltpu.VMEM)
    away = pl.BlockSpec(memory_space=pl.ANY)
    flat = lambda v: v.reshape(1, -1)
    moved = pl.pallas_call(
        functools.partial(kernel, scale_three, scale_four, tuple(table)),
        out_shape=(
            jax.ShapeDtypeStruct((8, 32, 512), BF16),
            jax.ShapeDtypeStruct((8, 64, 128), BF16),
            jax.ShapeDtypeStruct((8, 64, 128), BF16),
            jax.ShapeDtypeStruct((192, 512), F32),
        ),
        in_specs=[away] * 12,
        out_specs=(away, whole, whole, whole),
        scratch_shapes=list(table.values()),
        compiler_params=pltpu.CompilerParams(
            collective_id=0, has_side_effects=True, vmem_limit_bytes=60 << 20
        ),
        name="block_backward",
    )(
        block_input.reshape(8, 32, 512),
        kernel_three,
        flat(gain_three),
        expand_weight,
        project_weight,
        flat(layer_scale),
        flat(merge_gain),
        patch_weight,
        kernel_four,
        flat(gain_four),
        normed_cotangent.reshape(64, 1024),
        residual_cotangent.reshape(64, 1024),
    )
    shapes = (
        (8, 32, 512), (7, 7, 512), (1, 512), (16, 2048), (64, 512),
        (1, 512), (1, 512), (64, 1024), (7, 7, 1024), (1, 1024),
    )
    outs = pl.pallas_call(
        functools.partial(results_kernel, scale_three, scale_four),
        out_shape=tuple(
            jax.ShapeDtypeStruct(shape, F32 if n else BF16) for n, shape in enumerate(shapes)
        ),
        in_specs=[away, whole, whole, whole],
        out_specs=(away,) + (whole,) * 9,
        scratch_shapes=[pltpu.SemaphoreType.DMA((1,))],
        name="results",
    )(*moved)
    outs = list(outs)
    outs[0] = outs[0].reshape(1, 8, 32, 512)
    for n in (2, 5, 6, 9):
        outs[n] = outs[n].reshape(-1)
    return tuple(outs)


def solution(mesh):
    pixels = P(None, "row", "col", None)
    return jax.shard_map(
        body,
        mesh=mesh,
        in_specs=(pixels,) + (P(),) * 9 + (pixels, pixels),
        out_specs=(pixels, P(), P(), P("row", None), P("row", None), P(), P(), P("row", None), P(), P()),
        check_vma=False,
    )
```

```python
import functools
import math

import jax
import jax.numpy as jnp
from jax import lax
from jax.experimental import pallas as pl
from jax.experimental.pallas import tpu as pltpu
from jax.sharding import PartitionSpec as P

EPSILON = 1e-06
F32 = jnp.float32
BF16 = jnp.bfloat16
XS, YS, ZS, KS = 4, 4, 8, 2


class Place:
    def __init__(self):
        row, col = lax.axis_index("row"), lax.axis_index("col")
        self.row, self.col = row, col
        self.x, self.z = lax.rem(row, XS), lax.div(row, XS)
        self.k, self.y = lax.rem(col, KS), lax.div(col, KS)

    def near(self, down, right):
        rows, cols = XS * ZS, YS * KS
        return {
            "row": lax.rem(self.row + (down + rows), rows),
            "col": lax.rem(self.col + (right + cols), cols),
        }

    def core_peer(self):
        return {"row": self.row, "col": self.y * KS + (1 - self.k)}

    def y_peer(self, y):
        return {"row": self.row, "col": y * KS + self.k}

    def x_peer(self, x):
        return {"row": self.z * XS + x, "col": self.col}

    def z_peer(self, z):
        return {"row": z * XS + self.x, "col": self.col}

    def col_peer(self, col):
        return {"row": self.row, "col": col}


def remote(src, dst, send, recv, device):
    return pltpu.make_async_remote_copy(
        src_ref=src,
        dst_ref=dst,
        send_sem=send,
        recv_sem=recv,
        device_id=device,
        device_id_type=pl.DeviceIdType.MESH,
    )


class Exchange:
    def __init__(self, count, me, piece, slots, send, recv, peer):
        self.others = [lax.rem(me + d, count) for d in range(1, count)]
        self.copies = [
            remote(piece(p), slots.at[me], send.at[d], recv.at[me], peer(p))
            for d, p in enumerate(self.others)
        ]
        self.arrivals = [
            remote(piece(p), slots.at[p], send.at[d], recv.at[p], peer(p))
            for d, p in enumerate(self.others)
        ]

    def start(self):
        for copy in self.copies:
            copy.start()

    def wait_recv(self):
        for copy in self.arrivals:
            copy.wait_recv()

    def wait_send(self):
        for copy in self.copies:
            copy.wait_send()


W = 16
L = W + 6
CORNERS = ((1, 1), (1, -1), (-1, 1), (-1, -1))
HALOS = ("i3", "i4", "g4", "g3")
CHAINS = ("a1", "a2", "b1", "b2")
Y_FIRST = ("a1", "b2")
SMALL = (("e", 16), ("l", 8))


def halo_rows(name):
    return 8 if name.endswith("3") else 4


def scratch_table():
    vm, dma = pltpu.VMEM, pltpu.SemaphoreType.DMA
    packed = lambda pixels: vm((pixels * 8, 128), F32)
    table = {
        "w1": vm((512, 2048), BF16),
        "w2": vm((2048, 512), BF16),
        "wp": vm((2048, 1024), BF16),
        "wsem": dma((3,)),
        "f3": packed(14 * L), "g3": packed(14 * L), "m3": packed(8 * W), "gs3": packed(8 * W),
        "f4": packed(10 * L), "g4": packed(10 * L), "m4": packed(4 * W),
        "k3": packed(49), "k4": packed(49), "a3": packed(49), "a4": packed(49),
        "um": vm((256, 512), F32), "im": vm((256, 128), F32), "nb": vm((256, 512), BF16),
        "hb": vm((256, 2048), BF16), "sl": vm((256, 2048), F32), "br": vm((256, 512), F32),
        "us": vm((256, 512), F32), "is": vm((256, 128), F32), "pb": vm((64, 2048), BF16),
        "fg": vm((64, 1024), BF16), "gb": vm((256, 512), BF16),
        "gu": vm((256, 2048), BF16),
    }
    for name in HALOS:
        rows = halo_rows(name)
        table["c_" + name] = vm((rows, W, 8, 128), BF16)
        table["v_" + name] = vm((2, 3, W, 8, 128), BF16)
        table["h_" + name] = vm((2, rows, 3, 8, 128), BF16)
        table["d_" + name] = vm((4, 3, 3, 8, 128), BF16)
        table["s_" + name] = dma((8,))
        table["r_" + name] = dma((8,))
    for tag, rows in SMALL:
        table["small_" + tag] = vm((8 * rows, 512), F32)
        for name, shape in (
            ("got_", (YS * rows, 512)), ("acc_", (YS, rows, 512)), ("iny_", (YS, rows, 512)),
            ("xp_", (XS, rows, 128)), ("inx_", (XS, rows, 128)), ("z_", (ZS, rows, 128)),
            ("fin_", (XS, rows, 128)),
        ):
            table["sm" + name + tag] = vm(shape, F32)
        for name, count in (("k", 1), ("y", YS), ("x", XS), ("z", ZS), ("g", XS), ("c", YS * KS)):
            table["sm_s" + name + tag] = dma((count,))
            table["sm_r" + name + tag] = dma((count,))
    for half in ("a", "b"):
        table["sum3_" + half] = vm((ZS, 64, 128), F32)
        table["out4_" + half] = vm((ZS, 64, 128), BF16)
        table["in4_" + half] = vm((ZS, 64, 128), BF16)
        table["s4_" + half] = dma((ZS,))
        table["r4_" + half] = dma((ZS,))
    pieces = YS * XS * ZS
    for t in CHAINS:
        table["send_" + t] = vm((pieces, 32, 128), BF16)
        table["got_" + t] = vm((pieces, 32, 128), BF16)
        table["own_" + t] = vm((pieces, 32, 128), F32)
        table["out2_" + t] = vm((pieces, 32, 128), BF16)
        table["in2_" + t] = vm((4, 32, 32, 128), BF16)
        table["out3_" + t] = vm((32, 32, 128), BF16)
        table["in3_" + t] = vm((4, ZS, 32, 128), BF16)
        for stage, count in ((2, 4), (3, 4)):
            table["s%d_%s" % (stage, t)] = dma((count,))
            table["r%d_%s" % (stage, t)] = dma((count,))
    table.update(
        xin=vm((8, 32, 512), BF16), kin3=vm((7, 7, 512), F32), kin4=vm((7, 7, 1024), F32),
        gain3=vm((1, 512), F32), scale=vm((1, 512), F32), mgain=vm((1, 512), F32),
        gain4=vm((1, 1024), F32), cot=vm((64, 1024), BF16), res=vm((64, 1024), BF16),
        isem=dma((9,)), osem=dma((1,)), xout=vm((8, 32, 512), BF16),
        s1=dma((4,)), r1=dma((4,)),
        sfa=dma((YS * KS,)), rfa=dma((YS * KS,)), sfb=dma((YS * KS,)), rfb=dma((YS * KS,)),
    )
    return table


def pixels_at(ref, start, count):
    return ref[pl.ds(pl.multiple_of(start * 8, 8), count * 8), :].reshape(count, 8, 128)


def put_pixels(ref, start, value):
    count = value.shape[0]
    ref[pl.ds(pl.multiple_of(start * 8, 8), count * 8), :] = value.reshape(count * 8, 128)


def taps_in(weights, ref, groups):
    lanes = 8 // groups
    for p in range(7):
        line = weights[p]
        for g in range(groups):
            for s in range(lanes):
                ref[pl.ds(p * 56 + g * lanes + s, 7, stride=8), :] = line[
                    :, s * 128 : (s + 1) * 128
                ]


def quad(ref, length, row, column, g):
    dy, dx = divmod(g, 2)
    rows = []
    for yy in range(4):
        for h in range(2):
            start = ((row + 2 * yy + dy) * length + column + dx) * 8 + 4 * h
            rows.append(
                jnp.concatenate([ref[pl.ds(start + s, 8, stride=16), :] for s in range(4)], axis=1)
            )
    return jnp.concatenate(rows, axis=0)


def put_quad(ref, length, row, column, g, value):
    dy, dx = divmod(g, 2)
    for yy in range(4):
        for h in range(2):
            start = ((row + 2 * yy + dy) * length + column + dx) * 8 + 4 * h
            top = yy * 16 + h * 8
            for s in range(4):
                ref[pl.ds(start + s, 8, stride=16), :] = value[
                    top : top + 8, s * 128 : (s + 1) * 128
                ]


def flat_four(ref):
    return jnp.concatenate([ref[pl.ds(s, 64, stride=8), :] for s in range(8)], axis=1)


def put_four(ref, value):
    for i in range(4):
        for s in range(8):
            ref[pl.ds(((3 + i) * L + 3) * 8 + s, W, stride=8), :] = value[
                i * W : (i + 1) * W, s * 128 : (s + 1) * 128
            ]


def conv(framed, rows, taps, flip, out, base=None, part="own"):
    def gather_rows(i, low, high, acc):
        def over_p(p, acc):
            line = pixels_at(framed, (i + p) * L, L)
            for q in range(7):
                tap = (6 - p) * 7 + (6 - q) if flip else p * 7 + q
                acc = acc + line[q : q + W] * taps[pl.ds(pl.multiple_of(tap * 8, 8), 8), :]
            return acc

        return lax.fori_loop(low, high, over_p, acc)

    def own(i, carry):
        acc = jnp.zeros((W, 8, 128), F32) if base is None else pixels_at(base, i * W, W)
        acc = gather_rows(i, jnp.maximum(3 - i, 0), jnp.minimum(rows + 3 - i, 7), acc)
        put_pixels(out, i * W, acc)
        return carry

    def above(i, carry):
        put_pixels(out, i * W, gather_rows(i, 0, 3 - i, pixels_at(out, i * W, W)))
        return carry

    def below(i, carry):
        put_pixels(out, i * W, gather_rows(i, rows + 3 - i, 7, pixels_at(out, i * W, W)))
        return carry

    if part == "own":
        lax.fori_loop(0, rows, own, 0)
    else:
        lax.fori_loop(0, 3, above, 0)
        lax.fori_loop(rows - 3, rows, below, 0)


def tap_grads(framed, grads, rows, out):
    def over_p(p, carry):
        def over_rows(i, accs):
            line = pixels_at(framed, (i + p) * L, L)
            grad = pixels_at(grads, (i + 3) * L + 3, W)
            return tuple(acc + jnp.sum(line[q : q + W] * grad, axis=0) for q, acc in enumerate(accs))

        accs = lax.fori_loop(0, rows, over_rows, (jnp.zeros((8, 128), F32),) * 7)
        for q in range(7):
            put_pixels(out, p * 7 + q, accs[q][None])
        return carry

    lax.fori_loop(0, 7, over_p, 0)


class Halo:
    def __init__(self, at, t, name):
        self.rows = rows = halo_rows(name)
        self.at, self.t, self.name = at, t, name
        c, v, h, d = (t[key + name] for key in ("c_", "v_", "h_", "d_"))
        s, r = t["s_" + name], t["r_" + name]
        three = lambda way, size: pl.ds(size - 3, 3) if way > 0 else pl.ds(0, 3)
        self.copies = []
        for n, way in enumerate((1, -1)):
            self.copies.append(
                remote(c.at[three(way, rows)], v.at[n], s.at[n], r.at[n], at.near(way, 0))
            )
            self.copies.append(
                remote(c.at[:, three(way, W)], h.at[n], s.at[2 + n], r.at[2 + n], at.near(0, way))
            )
        for n, (down, right) in enumerate(CORNERS):
            self.copies.append(
                remote(
                    c.at[three(down, rows), three(right, W)], d.at[n], s.at[4 + n], r.at[4 + n],
                    at.near(down, right),
                )
            )

    def start(self, framed):
        c = self.t["c_" + self.name]

        def step(i, carry):
            c[i] = pixels_at(framed, (i + 3) * L + 3, W).astype(BF16)
            return carry

        lax.fori_loop(0, self.rows, step, 0)
        for copy in self.copies:
            copy.start()

    def wait_send(self):
        for copy in self.copies:
            copy.wait_send()

    def fill_sides(self, framed, lines):
        at, rows = self.at, self.rows
        h, d = self.t["h_" + self.name], self.t["d_" + self.name]
        one = lambda ok: jnp.where(ok, 1.0, 0.0).astype(F32)
        up, down = one(at.row > 0), one(at.row < XS * ZS - 1)
        left, right = one(at.col > 0), one(at.col < YS * KS - 1)
        for n, (side, start) in enumerate(((left, 0), (right, W + 3))):
            for i in lines:
                if i < 3:
                    value = d[n, i].astype(F32) * (side * up)
                elif i < rows + 3:
                    value = h[n, i - 3].astype(F32) * side
                else:
                    value = d[2 + n, i - rows - 3].astype(F32) * (side * down)
                if rows == 8:
                    inner = pixels_at(framed, i * L + (W if n == 0 else 3), 3)
                    first, second = (value, inner) if n == 0 else (inner, value)
                    value = jnp.concatenate([first[:, 4:8], second[:, 0:4]], axis=1)
                put_pixels(framed, i * L + start, value)

    def sides(self, framed):
        for copy in self.copies[1:4:2]:
            copy.wait_recv()
        self.fill_sides(framed, range(3, self.rows + 3))

    def ends(self, framed):
        for copy in self.copies[0:4:2] + self.copies[4:]:
            copy.wait_recv()
        at, rows = self.at, self.rows
        v = self.t["v_" + self.name]
        one = lambda ok: jnp.where(ok, 1.0, 0.0).astype(F32)
        up, down = one(at.row > 0), one(at.row < XS * ZS - 1)
        for n, (ok, first) in enumerate(((up, 0), (down, rows + 3))):
            for i in range(3):
                put_pixels(framed, (first + i) * L + 3, v[n, i].astype(F32) * ok)
        self.fill_sides(framed, [0, 1, 2, rows + 3, rows + 4, rows + 5])


class SmallSum:
    def __init__(self, at, t, tag, rows, total):
        self.at, self.t, self.tag, self.rows, self.total = at, t, tag, rows, total
        self.sends = []

    def ref(self, name):
        return self.t["sm" + name + self.tag]

    def sems(self, name):
        return self.ref("_s" + name), self.ref("_r" + name)

    def group(self, index, count=1):
        return pl.ds(pl.multiple_of(index * self.rows, 8), count * self.rows)

    def exchange(self, count, me, piece, slots, name, peer):
        result = Exchange(count, me, piece, slots, *self.sems(name), peer)
        result.start()
        self.sends.append(result)
        return result

    def core(self):
        at, got, (send, recv) = self.at, self.ref("got_"), self.sems("k")
        small = self.t["small_" + self.tag]
        self.crossing = [
            remote(
                small.at[self.group((1 - at.k) * YS, YS)], got, send.at[0], recv.at[0],
                at.core_peer(),
            )
        ]
        self.crossing[0].start()

    def over_y(self):
        at, acc, got = self.at, self.ref("acc_"), self.ref("got_")
        small = self.t["small_" + self.tag]
        self.crossing[0].wait_recv()
        for q in range(YS):
            part = slice(q * self.rows, (q + 1) * self.rows)
            acc[q] = small[self.group(at.k * YS + q), :] + got[part, :]
        self.y = self.exchange(YS, at.y, lambda p: acc.at[p], self.ref("iny_"), "y", at.y_peer)

    def over_x(self):
        at, pieces = self.at, self.ref("xp_")
        self.y.wait_recv()
        total = self.ref("acc_")[at.y]
        for p in self.y.others:
            total = total + self.ref("iny_")[p]
        for xx in range(XS):
            pieces[xx] = total[:, xx * 128 : (xx + 1) * 128]
        self.x = self.exchange(XS, at.x, lambda p: pieces.at[p], self.ref("inx_"), "x", at.x_peer)

    def over_z(self):
        at, slots = self.at, self.ref("z_")
        self.x.wait_recv()
        total = self.ref("xp_")[at.x]
        for p in self.x.others:
            total = total + self.ref("inx_")[p]
        slots[at.z] = total
        self.z = self.exchange(ZS, at.z, lambda p: slots.at[at.z], slots, "z", at.z_peer)

    def back_x(self):
        at, slots = self.at, self.ref("fin_")
        self.z.wait_recv()
        total = self.ref("z_")[0]
        for p in range(1, ZS):
            total = total + self.ref("z_")[p]
        slots[at.x] = total
        self.g = self.exchange(XS, at.x, lambda p: slots.at[at.x], slots, "g", at.x_peer)

    def back_col(self):
        at, total = self.at, self.total
        self.g.wait_recv()
        number = lambda c: lax.rem(c, KS) * YS + lax.div(c, KS)
        mine = self.group(number(at.col))
        total[mine, :] = jnp.concatenate([self.ref("fin_")[q] for q in range(XS)], axis=1)
        send, recv = self.sems("c")
        self.last, self.arrivals = [], []
        for d in range(1, YS * KS):
            c = lax.rem(at.col + d, YS * KS)
            self.last.append(
                remote(
                    total.at[mine], total.at[mine], send.at[d], recv.at[number(at.col)],
                    at.col_peer(c),
                )
            )
            self.arrivals.append(
                remote(
                    total.at[mine], total.at[self.group(number(c))], send.at[d],
                    recv.at[number(c)], at.col_peer(c),
                )
            )
        for copy in self.last:
            copy.start()

    def wait(self):
        for copy in self.arrivals:
            copy.wait_recv()

    def wait_send(self):
        for copy in self.crossing + self.last:
            copy.wait_send()
        for exchange in self.sends:
            exchange.wait_send()


def unit_of(values):
    mean_value = jnp.mean(values, axis=-1, keepdims=True)
    square = jnp.mean(values * values, axis=-1, keepdims=True)
    inverse = lax.rsqrt(square - mean_value * mean_value + EPSILON)
    return (values - mean_value) * inverse, inverse


def unit_back(grads, unit_values, inverse):
    return (
        grads
        - jnp.mean(grads, axis=-1, keepdims=True)
        - unit_values * jnp.mean(grads * unit_values, axis=-1, keepdims=True)
    ) * inverse


def by_rows(left, right):
    return lax.dot_general(left, right, (((0,), (0,)), ((), ())), preferred_element_type=F32)


def by_lanes(left, right):
    return lax.dot_general(left, right, (((1,), (1,)), ((), ())), preferred_element_type=F32)


def kernel(
    scale_three, scale_four, names,
    x_in, k3_in, gain3_in, w1_in, w2_in, scale_in, mgain_in, wp_in, k4_in, gain4_in, cot_in, res_in,
    input_o, fin_a, fin_b, early_o, late_o,
    *scratch,
):
    t = dict(zip(names, scratch))
    at = Place()
    x, y, z, k, col = at.x, at.y, at.z, at.k, at.col
    barrier = pltpu.get_barrier_semaphore()
    greeted = [at.col_peer(lax.rem(col + d, YS * KS)) for d in range(1, YS * KS)]
    greeted += [at.x_peer(lax.rem(x + d, XS)) for d in range(1, XS)]
    greeted += [at.z_peer(lax.rem(z + d, ZS)) for d in range(1, ZS)]
    greeted += [at.near(*way) for way in CORNERS + ((1, 0), (-1, 0))]
    for device in greeted:
        pl.semaphore_signal(barrier, inc=1, device_id=device, device_id_type=pl.DeviceIdType.MESH)
    params = [
        pltpu.make_async_copy(src, t[dst], t["isem"].at[i])
        for i, (src, dst) in enumerate(
            (
                (x_in, "xin"), (k3_in, "kin3"), (k4_in, "kin4"), (gain3_in, "gain3"),
                (scale_in, "scale"), (mgain_in, "mgain"), (gain4_in, "gain4"),
                (cot_in, "cot"), (res_in, "res"),
            )
        )
    ]
    weights = [
        pltpu.make_async_copy(src, t[dst], t["wsem"].at[i])
        for i, (src, dst) in enumerate(((w1_in, "w1"), (w2_in, "w2"), (wp_in, "wp")))
    ]
    for copy in params + weights:
        copy.start()
    for copy in params:
        copy.wait()
    xin, gain_three, layer_scale, merge_gain, gain_four, cot, res = (
        t[key] for key in ("xin", "gain3", "scale", "mgain", "gain4", "cot", "res")
    )

    f3, m3 = t["f3"], t["m3"]
    for i in range(8):
        line = xin[i].astype(F32)
        for h in range(2):
            for s in range(4):
                f3[pl.ds(((3 + i) * L + 3) * 8 + 4 * h + s, W, stride=8), :] = line[
                    h * W : (h + 1) * W, s * 128 : (s + 1) * 128
                ]
    taps_in(t["kin3"], t["k3"], 2)
    taps_in(t["kin4"], t["k4"], 1)
    pl.semaphore_wait(barrier, len(greeted))
    halo_i3 = Halo(at, t, "i3")
    halo_i3.start(f3)
    halo_i3.sides(f3)
    conv(f3, 8, t["k3"], False, m3)
    halo_i3.ends(f3)
    conv(f3, 8, t["k3"], False, m3, part="rest")
    for g in range(4):
        unit, inverse = unit_of(quad(m3, W, 0, 0, g))
        part = slice(g * 64, g * 64 + 64)
        t["um"][part, :] = unit
        t["im"][part, :] = jnp.broadcast_to(inverse, (64, 128))
        t["nb"][part, :] = (unit * gain_three[...]).astype(BF16)
    weights[0].wait()

    def expand(n, carry):
        lanes = pl.ds(pl.multiple_of(n * 256, 256), 256)
        upward = jnp.dot(t["nb"][...], t["w1"][:, lanes], preferred_element_type=F32)
        cumulative = 0.5 * (1.0 + lax.erf(upward * (1.0 / math.sqrt(2.0))))
        t["hb"][:, lanes] = (upward * cumulative).astype(BF16)
        t["sl"][:, lanes] = cumulative + upward * jnp.exp(-0.5 * upward * upward) * (
            1.0 / math.sqrt(2.0 * math.pi)
        )
        return carry

    lax.fori_loop(0, 8, expand, 0)
    weights[1].wait()
    t["br"][...] = jnp.dot(t["hb"][...], t["w2"][...], preferred_element_type=F32)
    for g in range(4):
        part = slice(g * 64, g * 64 + 64)
        summed = quad(f3, L, 3, 3, g) + layer_scale[...] * t["br"][part, :]
        unit, inverse = unit_of(summed)
        t["us"][part, :] = unit
        t["is"][part, :] = jnp.broadcast_to(inverse, (64, 128))
        t["pb"][:, g * 512 : (g + 1) * 512] = (unit * merge_gain[...]).astype(BF16)
    weights[2].wait()

    f4, g4, m4 = t["f4"], t["g4"], t["m4"]
    section_in = jnp.dot(t["pb"][...], t["wp"][...], preferred_element_type=F32)
    put_four(f4, section_in.astype(BF16).astype(F32))
    halo_i4 = Halo(at, t, "i4")
    halo_i4.start(f4)
    t["small_e"][...] = jnp.zeros((128, 512), F32)
    t["small_l"][...] = jnp.zeros((64, 512), F32)
    halo_i4.sides(f4)
    conv(f4, 4, t["k4"], False, m4)
    halo_i4.ends(f4)
    conv(f4, 4, t["k4"], False, m4, part="rest")
    unit_four, inverse_four = unit_of(flat_four(m4))
    cot_four = cot[...].astype(F32)
    gain_four_part = jnp.sum(cot_four * unit_four, axis=0, keepdims=True) * scale_four
    t["small_e"][112:113, :] = gain_four_part[:, 0:512]
    t["small_e"][113:114, :] = gain_four_part[:, 512:1024]
    put_four(g4, unit_back(cot_four * gain_four[...], unit_four, inverse_four))
    halo_g4 = Halo(at, t, "g4")
    halo_g4.start(g4)
    halo_g4.sides(g4)
    conv(g4, 4, t["k4"], True, m4)
    halo_g4.ends(g4)
    conv(g4, 4, t["k4"], True, m4, part="rest")
    t["fg"][...] = (res[...].astype(F32) + flat_four(m4)).astype(BF16)

    first = k == 0

    def split(index, row, even, odd, tag):
        here = slice(row, row + even.shape[0])
        t["send_" + tag][index, here, :] = jnp.where(first, odd, even).astype(BF16)
        t["own_" + tag][index, here, :] = jnp.where(first, even, odd)

    def products_a(zz, carry):
        lanes = pl.ds(pl.multiple_of(zz * 256, 256), 256)
        out = by_rows(t["pb"][:, lanes], t["fg"][...])
        for q in range(YS):
            for xx in range(XS):
                block = out[xx * 64 : (xx + 1) * 64, q * 256 : (q + 1) * 256]
                split(q * (XS * ZS) + xx * ZS + zz, 0, block[:32, :128], block[:32, 128:], "a1")
                split(xx * (YS * ZS) + q * ZS + zz, 0, block[32:, :128], block[32:, 128:], "a2")
        return carry

    lax.fori_loop(0, ZS, products_a, 0)
    core = {}

    def cross(tag):
        n = CHAINS.index(tag)
        core[tag] = remote(
            t["send_" + tag], t["got_" + tag], t["s1"].at[n], t["r1"].at[n], at.core_peer()
        )
        core[tag].start()

    cross("a1")
    cross("a2")
    early, late = (
        SmallSum(at, t, tag, rows, total) for (tag, rows), total in zip(SMALL, (early_o, late_o))
    )
    tap_grads(f4, g4, 4, t["a4"])
    for s in range(4):
        lanes = slice(s * 128, (s + 1) * 128)
        t["small_e"][0:49, lanes] = t["a4"][pl.ds(s, 49, stride=8), :] * scale_four
        t["small_e"][56:105, lanes] = t["a4"][pl.ds(4 + s, 49, stride=8), :] * scale_four
    early.core()

    merge_part = scale_part = jnp.zeros((1, 512), F32)
    for g in range(4):
        part = slice(g * 64, g * 64 + 64)
        unit = t["us"][part, :]
        grad_merged = by_lanes(t["fg"][...], t["wp"][g * 512 : (g + 1) * 512, :])
        merge_part = merge_part + jnp.sum(grad_merged * unit, axis=0, keepdims=True)
        grad = unit_back(grad_merged * merge_gain[...], unit, t["is"][part, 0:1])
        scale_part = scale_part + jnp.sum(grad * t["br"][part, :], axis=0, keepdims=True)
        put_quad(t["gs3"], W, 0, 0, g, grad)
        t["gb"][part, :] = (layer_scale[...] * grad).astype(BF16)
    t["small_l"][57:58, :] = scale_part * scale_three
    t["small_l"][58:59, :] = merge_part * scale_three

    def products_b(zz, carry):
        lanes = pl.ds(pl.multiple_of(zz * 256, 256), 256)
        out = by_rows(t["hb"][:, lanes], t["gb"][...])
        for q in range(YS):
            for xx in range(XS):
                block = out[xx * 64 : (xx + 1) * 64, q * 128 : (q + 1) * 128]
                split(xx * (YS * ZS) + q * ZS + zz, 0, block[:32], block[32:], "b1")
        return carry

    lax.fori_loop(0, ZS, products_b, 0)
    cross("b1")

    per2 = 32

    def second(tag):
        me, peer = (y, at.y_peer) if tag in Y_FIRST else (x, at.x_peer)
        core[tag].wait_recv()
        exchange = Exchange(
            4, me, lambda p: t["out2_" + tag].at[pl.ds(p * per2, per2)], t["in2_" + tag],
            t["s2_" + tag], t["r2_" + tag], peer,
        )
        own, got, out = t["own_" + tag], t["got_" + tag], t["out2_" + tag]
        for d, p in enumerate(exchange.others):

            def step(i, carry, p=p):
                j = p * per2 + i
                out[j] = (own[j] + got[j].astype(F32)).astype(BF16)
                return carry

            lax.fori_loop(0, per2, step, 0, unroll=4)
            exchange.copies[d].start()
        return exchange

    seconds = {"a1": second("a1"), "a2": second("a2")}
    early.over_y()

    def narrow(n, carry):
        lanes = pl.ds(pl.multiple_of(n * 256, 256), 256)
        grad_hidden = by_lanes(t["gb"][...], t["w2"][lanes, :])
        t["gu"][:, lanes] = (grad_hidden * t["sl"][:, lanes]).astype(BF16)
        return carry

    lax.fori_loop(0, 8, narrow, 0)

    seconds["b1"] = second("b1")
    early.over_x()

    grad_normed = by_lanes(t["gu"][...], t["w1"][...])
    gain_part = jnp.zeros((1, 512), F32)
    g3 = t["g3"]
    for g in range(4):
        part = slice(g * 64, g * 64 + 64)
        unit, grad = t["um"][part, :], grad_normed[part, :]
        gain_part = gain_part + jnp.sum(grad * unit, axis=0, keepdims=True)
        grad = unit_back(grad * gain_three[...], unit, t["im"][part, 0:1])
        put_quad(g3, L, 3, 3, g, grad.astype(BF16).astype(F32))
    t["small_l"][56:57, :] = gain_part * scale_three
    halo_g3 = Halo(at, t, "g3")
    halo_g3.start(g3)
    early.over_z()

    def products_e(pair, carry):
        lanes = pl.ds(pl.multiple_of(pair * 128, 128), 128)
        for q in range(YS):
            out = by_rows(t["nb"][:, lanes], t["gu"][:, q * 512 : (q + 1) * 512])
            for hz in range(2):
                for xx in range(XS):
                    rows = slice(hz * 64 + xx * 16, hz * 64 + xx * 16 + 16)
                    for half in range(2):
                        lane = half * 128
                        split(
                            q * (XS * ZS) + xx * ZS + 2 * pair + hz, 16 * half,
                            out[rows, lane : lane + 128], out[rows, 256 + lane : 384 + lane], "b2",
                        )
        return carry

    lax.fori_loop(0, ZS // 2, products_e, 0)
    cross("b2")

    def third(tag):
        before = seconds[tag]
        me, me3, peer = (y, x, at.x_peer) if tag in Y_FIRST else (x, y, at.y_peer)
        before.wait_recv()
        own, got, slots = t["own_" + tag], t["got_" + tag], t["in2_" + tag]
        out = t["out3_" + tag]
        here = pl.ds((int(tag[1]) - 1) * 32, 32)
        exchange = Exchange(
            4, me3, lambda p: out.at[pl.ds(p * ZS, ZS)], t["in3_" + tag],
            t["s3_" + tag], t["r3_" + tag], peer,
        )

        def total_of(i):
            j = me * per2 + i
            acc = own[j] + got[j].astype(F32)
            for p in before.others:
                acc = acc + slots[p, i].astype(F32)
            return acc

        for d, p in enumerate(exchange.others):

            def step(i, carry, p=p):
                j = p * ZS + i
                out[j] = total_of(j).astype(BF16)
                return carry

            lax.fori_loop(0, ZS, step, 0, unroll=4)
            exchange.copies[d].start()

        def keep(i, carry):
            t["sum3_" + tag[0]][i, here, :] = total_of(me3 * ZS + i)
            return carry

        lax.fori_loop(0, ZS, keep, 0, unroll=4)
        return exchange

    def fourth(tag):
        before = thirds[tag]
        before.wait_recv()
        slots = t["in3_" + tag]
        here = pl.ds((int(tag[1]) - 1) * 32, 32)

        def step(i, carry):
            acc = t["sum3_" + tag[0]][i, here, :]
            for p in before.others:
                acc = acc + slots[p, i].astype(F32)
            t["sum3_" + tag[0]][i, here, :] = acc
            t["out4_" + tag[0]][i, here, :] = acc.astype(BF16)
            return carry

        lax.fori_loop(0, ZS, step, 0, unroll=4)

    def over_z(half):
        exchange = Exchange(
            ZS, z, lambda p: t["out4_" + half].at[p], t["in4_" + half],
            t["s4_" + half], t["r4_" + half], at.z_peer,
        )
        exchange.start()
        return exchange

    def collect(half, exchange, fin):
        exchange.wait_recv()
        acc = t["sum3_" + half][z]
        for p in exchange.others:
            acc = acc + t["in4_" + half][p].astype(F32)
        fin[col] = acc.astype(BF16)
        gather = Exchange(
            YS * KS, col, lambda p: fin.at[col], fin, t["sf" + half], t["rf" + half], at.col_peer
        )
        gather.start()
        return gather

    thirds = {"a1": third("a1"), "a2": third("a2")}
    seconds["b2"] = second("b2")

    tap_grads(f3, g3, 8, t["a3"])
    for s in range(4):
        t["small_l"][0:49, s * 128 : (s + 1) * 128] = (
            t["a3"][pl.ds(s, 49, stride=8), :] + t["a3"][pl.ds(4 + s, 49, stride=8), :]
        ) * scale_three
    late.core()
    early.back_x()
    halo_g3.sides(g3)
    conv(g3, 8, t["k3"], True, m3, t["gs3"])
    late.over_y()
    fourth("a1")
    fourth("a2")
    z_a = over_z("a")
    halo_g3.ends(g3)
    conv(g3, 8, t["k3"], True, m3, part="rest")
    late.over_x()
    early.back_col()
    thirds["b1"] = third("b1")

    def leave(i, carry):
        for h in range(2):
            row = jnp.concatenate(
                [m3[pl.ds(i * (W * 8) + 4 * h + s, W, stride=8), :] for s in range(4)], axis=1
            )
            t["xout"][i, h * W : (h + 1) * W, :] = row.astype(BF16)
        return carry

    lax.fori_loop(0, 8, leave, 0)
    out_copy = pltpu.make_async_copy(t["xout"], input_o, t["osem"].at[0])
    out_copy.start()
    late.over_z()
    thirds["b2"] = third("b2")
    gather_a = collect("a", z_a, fin_a)
    late.back_x()
    fourth("b1")
    fourth("b2")
    z_b = over_z("b")
    late.back_col()
    gather_b = collect("b", z_b, fin_b)
    early.wait()
    gather_a.wait_recv()
    late.wait()
    gather_b.wait_recv()
    out_copy.wait()

    for tag in CHAINS:
        core[tag].wait_send()
    for tag in CHAINS:
        for stage in (seconds, thirds):
            stage[tag].wait_send()
    for exchange in (
        halo_i3, halo_i4, halo_g4, halo_g3, z_a, z_b, gather_a, gather_b, early, late,
    ):
        exchange.wait_send()


def results_kernel(
    scale_three, scale_four, input_i, fin_a, fin_b, early, late,
    input_o, k3_o, gain3_o, expand_o, project_o, scale_o, merge_o, patch_o, k4_o, gain4_o,
):
    input_o[...] = input_i[...]
    for c in range(YS * KS):
        q, kk = divmod(c, KS)
        patch_o[:, c * 128 : (c + 1) * 128] = fin_a[c].astype(F32) * scale_four
        project_o[kk * 32 : (kk + 1) * 32, q * 128 : (q + 1) * 128] = (
            fin_b[c, 0:32].astype(F32) * scale_three
        )
        for half in range(2):
            lane = c * 256 + half * 128
            expand_o[:, lane : lane + 128] = (
                fin_b[c, 32 + half * 16 : 48 + half * 16].astype(F32) * scale_three
            )
    for p in range(7):
        k3_o[p] = late[7 * p : 7 * p + 7, :]
        k4_o[p, :, 0:512] = early[7 * p : 7 * p + 7, :]
        k4_o[p, :, 512:1024] = early[56 + 7 * p : 63 + 7 * p, :]
    gain3_o[...] = late[56:57, :]
    scale_o[...] = late[57:58, :]
    merge_o[...] = late[58:59, :]
    gain4_o[:, 0:512] = early[112:113, :]
    gain4_o[:, 512:1024] = early[113:114, :]


def body(
    block_input,
    kernel_three,
    gain_three,
    expand_weight,
    project_weight,
    layer_scale,
    merge_gain,
    patch_weight,
    kernel_four,
    gain_four,
    normed_cotangent,
    residual_cotangent,
):
    devices = lax.axis_size("row") * lax.axis_size("col")
    scale_three = 1.0 / math.sqrt(256 * devices)
    scale_four = 1.0 / math.sqrt(64 * devices)
    table = scratch_table()
    whole = pl.BlockSpec(memory_space=pltpu.VMEM)
    away = pl.BlockSpec(memory_space=pl.ANY)
    flat = lambda v: v.reshape(1, -1)
    moved = pl.pallas_call(
        functools.partial(kernel, scale_three, scale_four, tuple(table)),
        out_shape=(
            jax.ShapeDtypeStruct((8, 32, 512), BF16),
            jax.ShapeDtypeStruct((8, 64, 128), BF16),
            jax.ShapeDtypeStruct((8, 64, 128), BF16),
            jax.ShapeDtypeStruct((128, 512), F32),
            jax.ShapeDtypeStruct((64, 512), F32),
        ),
        in_specs=[away] * 12,
        out_specs=(away,) + (whole,) * 4,
        scratch_shapes=list(table.values()),
        compiler_params=pltpu.CompilerParams(
            collective_id=0, has_side_effects=True, vmem_limit_bytes=60 << 20
        ),
        name="block_backward",
    )(
        block_input.reshape(8, 32, 512),
        kernel_three,
        flat(gain_three),
        expand_weight,
        project_weight,
        flat(layer_scale),
        flat(merge_gain),
        patch_weight,
        kernel_four,
        flat(gain_four),
        normed_cotangent.reshape(64, 1024),
        residual_cotangent.reshape(64, 1024),
    )
    shapes = (
        (8, 32, 512), (7, 7, 512), (1, 512), (16, 2048), (64, 512),
        (1, 512), (1, 512), (64, 1024), (7, 7, 1024), (1, 1024),
    )
    outs = pl.pallas_call(
        functools.partial(results_kernel, scale_three, scale_four),
        out_shape=tuple(
            jax.ShapeDtypeStruct(shape, F32 if n else BF16) for n, shape in enumerate(shapes)
        ),
        in_specs=[whole] * 5,
        out_specs=(whole,) * 10,
        compiler_params=pltpu.CompilerParams(vmem_limit_bytes=16 << 20),
        name="results",
    )(*moved)
    outs = list(outs)
    outs[0] = outs[0].reshape(1, 8, 32, 512)
    for n in (2, 5, 6, 9):
        outs[n] = outs[n].reshape(-1)
    return tuple(outs)


def solution(mesh):
    pixels = P(None, "row", "col", None)
    return jax.shard_map(
        body,
        mesh=mesh,
        in_specs=(pixels,) + (P(),) * 9 + (pixels, pixels),
        out_specs=(pixels, P(), P(), P("row", None), P("row", None), P(), P(), P("row", None), P(), P()),
        check_vma=False,
    )
```

```python
import functools
import math

import jax
import jax.numpy as jnp
from jax import lax
from jax.experimental import pallas as pl
from jax.experimental.pallas import tpu as pltpu
from jax.sharding import PartitionSpec as P

EPSILON = 1e-06
F32 = jnp.float32
BF16 = jnp.bfloat16
XS, YS, ZS, KS = 4, 4, 8, 2


class Place:
    def __init__(self):
        row, col = lax.axis_index("row"), lax.axis_index("col")
        self.row, self.col = row, col
        self.x, self.z = lax.rem(row, XS), lax.div(row, XS)
        self.k, self.y = lax.rem(col, KS), lax.div(col, KS)

    def near(self, down, right):
        rows, cols = XS * ZS, YS * KS
        return {
            "row": lax.rem(self.row + (down + rows), rows),
            "col": lax.rem(self.col + (right + cols), cols),
        }

    def core_peer(self):
        return {"row": self.row, "col": self.y * KS + (1 - self.k)}

    def y_peer(self, y):
        return {"row": self.row, "col": y * KS + self.k}

    def x_peer(self, x):
        return {"row": self.z * XS + x, "col": self.col}

    def z_peer(self, z):
        return {"row": z * XS + self.x, "col": self.col}

    def col_peer(self, col):
        return {"row": self.row, "col": col}


def remote(src, dst, send, recv, device):
    return pltpu.make_async_remote_copy(
        src_ref=src,
        dst_ref=dst,
        send_sem=send,
        recv_sem=recv,
        device_id=device,
        device_id_type=pl.DeviceIdType.MESH,
    )


class Exchange:
    def __init__(self, count, me, piece, slots, send, recv, peer):
        far_first = sorted(range(1, count), key=lambda d: -min(d, count - d))
        self.others = [lax.rem(me + d, count) for d in far_first]
        self.copies = [
            remote(piece(p), slots.at[me], send.at[d], recv.at[me], peer(p))
            for d, p in enumerate(self.others)
        ]
        self.arrivals = [
            remote(piece(p), slots.at[p], send.at[d], recv.at[p], peer(p))
            for d, p in enumerate(self.others)
        ]

    def start(self):
        for copy in self.copies:
            copy.start()

    def wait_recv(self):
        for copy in self.arrivals:
            copy.wait_recv()

    def wait_send(self):
        for copy in self.copies:
            copy.wait_send()


W = 16
L = W + 6
CORNERS = ((1, 1), (1, -1), (-1, 1), (-1, -1))
HALOS = ("i3", "i4", "g4", "g3")
CHAINS = {"a1": 32, "a2": 32, "b1": 16, "b2": 16, "c1": 16, "c2": 16}
Y_FIRST = ("a1", "b1", "c1")
Z_EARLY = ("a1", "a2")
SMALL = (("e", 16), ("l", 8))


def halo_rows(name):
    return 8 if name.endswith("3") else 4


def scratch_table():
    vm, dma = pltpu.VMEM, pltpu.SemaphoreType.DMA
    packed = lambda pixels: vm((pixels * 8, 128), F32)
    table = {
        "w1": vm((512, 2048), BF16),
        "w2": vm((2048, 512), BF16),
        "wp": vm((2048, 1024), BF16),
        "wsem": dma((3,)),
        "f3": packed(14 * L), "g3": packed(14 * L), "m3": packed(8 * W), "gs3": packed(8 * W),
        "f4": packed(10 * L), "g4": packed(10 * L), "m4": packed(4 * W),
        "k3": packed(49), "k4": packed(49), "a3": packed(49), "a4": packed(49),
        "um": vm((256, 512), F32), "im": vm((256, 128), F32), "nb": vm((256, 512), BF16),
        "hb": vm((256, 2048), BF16), "sl": vm((256, 2048), F32), "br": vm((256, 512), F32),
        "us": vm((256, 512), F32), "is": vm((256, 128), F32), "pb": vm((64, 2048), BF16),
        "fg": vm((64, 1024), BF16), "gb": vm((256, 512), BF16),
        "gu": vm((256, 2048), BF16),
    }
    for name in HALOS:
        rows = halo_rows(name)
        table["c_" + name] = vm((rows, W, 8, 128), BF16)
        table["v_" + name] = vm((2, 3, W, 8, 128), BF16)
        table["h_" + name] = vm((2, rows, 3, 8, 128), BF16)
        table["d_" + name] = vm((4, 3, 3, 8, 128), BF16)
        table["s_" + name] = dma((8,))
        table["r_" + name] = dma((8,))
    for tag, rows in SMALL:
        table["small_" + tag] = vm((8 * rows, 512), F32)
        for name, shape in (
            ("got_", (YS * rows, 512)), ("acc_", (YS, rows, 512)), ("iny_", (YS, rows, 512)),
            ("xp_", (XS, rows, 128)), ("inx_", (XS, rows, 128)), ("z_", (ZS, rows, 128)),
            ("fin_", (XS, rows, 128)),
        ):
            table["sm" + name + tag] = vm(shape, F32)
        for name, count in (("k", 1), ("y", YS), ("x", XS), ("z", ZS), ("g", XS), ("c", YS * KS)):
            table["sm_s" + name + tag] = dma((count,))
            table["sm_r" + name + tag] = dma((count,))
    pieces = YS * XS * ZS
    for t, deep in CHAINS.items():
        table["send_" + t] = vm((pieces, deep, 128), BF16)
        table["got_" + t] = vm((pieces, deep, 128), BF16)
        table["own_" + t] = vm((pieces, deep, 128), F32)
        table["out2_" + t] = vm((pieces, deep, 128), BF16)
        table["in2_" + t] = vm((4, 32, deep, 128), BF16)
        table["out3_" + t] = vm((32, deep, 128), BF16)
        third = ZS if t in Z_EARLY else 4
        table["in3_" + t] = vm((third, 32 // third, deep, 128), BF16)
        table["sum3_" + t] = vm((32 // third, deep, 128), F32)
        table["out4_" + t] = vm((32 // third, deep, 128), BF16)
        table["in4_" + t] = vm((32 // third, deep, 128), BF16)
        for stage, count in ((2, 4), (3, third), (4, 32 // third)):
            table["s%d_%s" % (stage, t)] = dma((count,))
            table["r%d_%s" % (stage, t)] = dma((count,))
    table.update(
        xin=vm((8, 32, 512), BF16), kin3=vm((7, 7, 512), F32), kin4=vm((7, 7, 1024), F32),
        gain3=vm((1, 512), F32), scale=vm((1, 512), F32), mgain=vm((1, 512), F32),
        gain4=vm((1, 1024), F32), cot=vm((64, 1024), BF16), res=vm((64, 1024), BF16),
        isem=dma((9,)), osem=dma((1,)), xout=vm((8, 32, 512), BF16),
        s1=dma((6,)), r1=dma((6,)),
        sfa=dma((YS * KS,)), rfa=dma((YS * KS,)), sfb=dma((YS * KS,)), rfb=dma((YS * KS,)),
    )
    return table


def pixels_at(ref, start, count):
    return ref[pl.ds(pl.multiple_of(start * 8, 8), count * 8), :].reshape(count, 8, 128)


def put_pixels(ref, start, value):
    count = value.shape[0]
    ref[pl.ds(pl.multiple_of(start * 8, 8), count * 8), :] = value.reshape(count * 8, 128)


def taps_in(weights, ref, groups):
    lanes = 8 // groups
    for p in range(7):
        line = weights[p]
        for g in range(groups):
            for s in range(lanes):
                ref[pl.ds(p * 56 + g * lanes + s, 7, stride=8), :] = line[
                    :, s * 128 : (s + 1) * 128
                ]


def quad(ref, length, row, column, g):
    dy, dx = divmod(g, 2)
    rows = []
    for yy in range(4):
        for h in range(2):
            start = ((row + 2 * yy + dy) * length + column + dx) * 8 + 4 * h
            rows.append(
                jnp.concatenate([ref[pl.ds(start + s, 8, stride=16), :] for s in range(4)], axis=1)
            )
    return jnp.concatenate(rows, axis=0)


def put_quad(ref, length, row, column, g, value):
    dy, dx = divmod(g, 2)
    for yy in range(4):
        for h in range(2):
            start = ((row + 2 * yy + dy) * length + column + dx) * 8 + 4 * h
            top = yy * 16 + h * 8
            for s in range(4):
                ref[pl.ds(start + s, 8, stride=16), :] = value[
                    top : top + 8, s * 128 : (s + 1) * 128
                ]


def flat_four(ref):
    return jnp.concatenate([ref[pl.ds(s, 64, stride=8), :] for s in range(8)], axis=1)


def put_four(ref, value):
    for i in range(4):
        for s in range(8):
            ref[pl.ds(((3 + i) * L + 3) * 8 + s, W, stride=8), :] = value[
                i * W : (i + 1) * W, s * 128 : (s + 1) * 128
            ]


def conv(framed, rows, taps, flip, out, base=None, part="own"):
    def gather_rows(i, low, high, acc):
        def over_p(p, acc):
            line = pixels_at(framed, (i + p) * L, L)
            for q in range(7):
                tap = (6 - p) * 7 + (6 - q) if flip else p * 7 + q
                acc = acc + line[q : q + W] * taps[pl.ds(pl.multiple_of(tap * 8, 8), 8), :]
            return acc

        return lax.fori_loop(low, high, over_p, acc)

    def own(i, carry):
        acc = jnp.zeros((W, 8, 128), F32) if base is None else pixels_at(base, i * W, W)
        acc = gather_rows(i, jnp.maximum(3 - i, 0), jnp.minimum(rows + 3 - i, 7), acc)
        put_pixels(out, i * W, acc)
        return carry

    def above(i, carry):
        put_pixels(out, i * W, gather_rows(i, 0, 3 - i, pixels_at(out, i * W, W)))
        return carry

    def below(i, carry):
        put_pixels(out, i * W, gather_rows(i, rows + 3 - i, 7, pixels_at(out, i * W, W)))
        return carry

    if part == "own":
        lax.fori_loop(0, rows, own, 0)
    else:
        lax.fori_loop(0, 3, above, 0)
        lax.fori_loop(rows - 3, rows, below, 0)


def tap_grads(framed, grads, rows, out):
    def over_p(p, carry):
        def over_rows(i, accs):
            line = pixels_at(framed, (i + p) * L, L)
            grad = pixels_at(grads, (i + 3) * L + 3, W)
            return tuple(acc + jnp.sum(line[q : q + W] * grad, axis=0) for q, acc in enumerate(accs))

        accs = lax.fori_loop(0, rows, over_rows, (jnp.zeros((8, 128), F32),) * 7)
        for q in range(7):
            put_pixels(out, p * 7 + q, accs[q][None])
        return carry

    lax.fori_loop(0, 7, over_p, 0)


class Halo:
    def __init__(self, at, t, name):
        self.rows = rows = halo_rows(name)
        self.at, self.t, self.name = at, t, name
        c, v, h, d = (t[key + name] for key in ("c_", "v_", "h_", "d_"))
        s, r = t["s_" + name], t["r_" + name]
        three = lambda way, size: pl.ds(size - 3, 3) if way > 0 else pl.ds(0, 3)
        self.copies = []
        for n, way in enumerate((1, -1)):
            self.copies.append(
                remote(c.at[three(way, rows)], v.at[n], s.at[n], r.at[n], at.near(way, 0))
            )
            self.copies.append(
                remote(c.at[:, three(way, W)], h.at[n], s.at[2 + n], r.at[2 + n], at.near(0, way))
            )
        for n, (down, right) in enumerate(CORNERS):
            self.copies.append(
                remote(
                    c.at[three(down, rows), three(right, W)], d.at[n], s.at[4 + n], r.at[4 + n],
                    at.near(down, right),
                )
            )

    def start(self, framed):
        c = self.t["c_" + self.name]

        def step(i, carry):
            c[i] = pixels_at(framed, (i + 3) * L + 3, W).astype(BF16)
            return carry

        lax.fori_loop(0, self.rows, step, 0)
        for copy in self.copies:
            copy.start()

    def wait_send(self):
        for copy in self.copies:
            copy.wait_send()

    def fill_sides(self, framed, lines):
        at, rows = self.at, self.rows
        h, d = self.t["h_" + self.name], self.t["d_" + self.name]
        one = lambda ok: jnp.where(ok, 1.0, 0.0).astype(F32)
        up, down = one(at.row > 0), one(at.row < XS * ZS - 1)
        left, right = one(at.col > 0), one(at.col < YS * KS - 1)
        for n, (side, start) in enumerate(((left, 0), (right, W + 3))):
            for i in lines:
                if i < 3:
                    value = d[n, i].astype(F32) * (side * up)
                elif i < rows + 3:
                    value = h[n, i - 3].astype(F32) * side
                else:
                    value = d[2 + n, i - rows - 3].astype(F32) * (side * down)
                if rows == 8:
                    inner = pixels_at(framed, i * L + (W if n == 0 else 3), 3)
                    first, second = (value, inner) if n == 0 else (inner, value)
                    value = jnp.concatenate([first[:, 4:8], second[:, 0:4]], axis=1)
                put_pixels(framed, i * L + start, value)

    def sides(self, framed):
        for copy in self.copies[1:4:2]:
            copy.wait_recv()
        self.fill_sides(framed, range(3, self.rows + 3))

    def ends(self, framed):
        for copy in self.copies[0:4:2] + self.copies[4:]:
            copy.wait_recv()
        at, rows = self.at, self.rows
        v = self.t["v_" + self.name]
        one = lambda ok: jnp.where(ok, 1.0, 0.0).astype(F32)
        up, down = one(at.row > 0), one(at.row < XS * ZS - 1)
        for n, (ok, first) in enumerate(((up, 0), (down, rows + 3))):
            for i in range(3):
                put_pixels(framed, (first + i) * L + 3, v[n, i].astype(F32) * ok)
        self.fill_sides(framed, [0, 1, 2, rows + 3, rows + 4, rows + 5])


class SmallSum:
    def __init__(self, at, t, tag, rows, total):
        self.at, self.t, self.tag, self.rows, self.total = at, t, tag, rows, total
        self.sends = []

    def ref(self, name):
        return self.t["sm" + name + self.tag]

    def sems(self, name):
        return self.ref("_s" + name), self.ref("_r" + name)

    def group(self, index, count=1):
        return pl.ds(pl.multiple_of(index * self.rows, 8), count * self.rows)

    def exchange(self, count, me, piece, slots, name, peer):
        result = Exchange(count, me, piece, slots, *self.sems(name), peer)
        result.start()
        self.sends.append(result)
        return result

    def core(self):
        at, got, (send, recv) = self.at, self.ref("got_"), self.sems("k")
        small = self.t["small_" + self.tag]
        self.crossing = [
            remote(
                small.at[self.group((1 - at.k) * YS, YS)], got, send.at[0], recv.at[0],
                at.core_peer(),
            )
        ]
        self.crossing[0].start()

    def over_y(self):
        at, acc, got = self.at, self.ref("acc_"), self.ref("got_")
        small = self.t["small_" + self.tag]
        self.crossing[0].wait_recv()
        for q in range(YS):
            part = slice(q * self.rows, (q + 1) * self.rows)
            acc[q] = small[self.group(at.k * YS + q), :] + got[part, :]
        self.y = self.exchange(YS, at.y, lambda p: acc.at[p], self.ref("iny_"), "y", at.y_peer)

    def over_x(self):
        at, pieces = self.at, self.ref("xp_")
        self.y.wait_recv()
        total = self.ref("acc_")[at.y]
        for p in self.y.others:
            total = total + self.ref("iny_")[p]
        for xx in range(XS):
            pieces[xx] = total[:, xx * 128 : (xx + 1) * 128]
        self.x = self.exchange(XS, at.x, lambda p: pieces.at[p], self.ref("inx_"), "x", at.x_peer)

    def over_z(self):
        at, slots = self.at, self.ref("z_")
        self.x.wait_recv()
        total = self.ref("xp_")[at.x]
        for p in self.x.others:
            total = total + self.ref("inx_")[p]
        slots[at.z] = total
        self.z = self.exchange(ZS, at.z, lambda p: slots.at[at.z], slots, "z", at.z_peer)

    def back_x(self):
        at, slots = self.at, self.ref("fin_")
        self.z.wait_recv()
        total = self.ref("z_")[0]
        for p in range(1, ZS):
            total = total + self.ref("z_")[p]
        slots[at.x] = total
        self.g = self.exchange(XS, at.x, lambda p: slots.at[at.x], slots, "g", at.x_peer)

    def back_col(self):
        at, total = self.at, self.total
        self.g.wait_recv()
        number = lambda c: lax.rem(c, KS) * YS + lax.div(c, KS)
        mine = self.group(number(at.col))
        total[mine, :] = jnp.concatenate([self.ref("fin_")[q] for q in range(XS)], axis=1)
        send, recv = self.sems("c")
        self.last, self.arrivals = [], []
        for d in range(1, YS * KS):
            c = lax.rem(at.col + d, YS * KS)
            self.last.append(
                remote(
                    total.at[mine], total.at[mine], send.at[d], recv.at[number(at.col)],
                    at.col_peer(c),
                )
            )
            self.arrivals.append(
                remote(
                    total.at[mine], total.at[self.group(number(c))], send.at[d],
                    recv.at[number(c)], at.col_peer(c),
                )
            )
        for copy in self.last:
            copy.start()

    def wait(self):
        for copy in self.arrivals:
            copy.wait_recv()

    def wait_send(self):
        for copy in self.crossing + self.last:
            copy.wait_send()
        for exchange in self.sends:
            exchange.wait_send()


def unit_of(values):
    mean_value = jnp.mean(values, axis=-1, keepdims=True)
    square = jnp.mean(values * values, axis=-1, keepdims=True)
    inverse = lax.rsqrt(square - mean_value * mean_value + EPSILON)
    return (values - mean_value) * inverse, inverse


def unit_back(grads, unit_values, inverse):
    return (
        grads
        - jnp.mean(grads, axis=-1, keepdims=True)
        - unit_values * jnp.mean(grads * unit_values, axis=-1, keepdims=True)
    ) * inverse


def by_rows(left, right):
    return lax.dot_general(left, right, (((0,), (0,)), ((), ())), preferred_element_type=F32)


def by_lanes(left, right):
    return lax.dot_general(left, right, (((1,), (1,)), ((), ())), preferred_element_type=F32)


def kernel(
    scale_three, scale_four, names,
    x_in, k3_in, gain3_in, w1_in, w2_in, scale_in, mgain_in, wp_in, k4_in, gain4_in, cot_in, res_in,
    input_o, fin_a, fin_b, early_o, late_o,
    *scratch,
):
    t = dict(zip(names, scratch))
    at = Place()
    x, y, z, k, col = at.x, at.y, at.z, at.k, at.col
    barrier = pltpu.get_barrier_semaphore()
    greeted = [at.col_peer(lax.rem(col + d, YS * KS)) for d in range(1, YS * KS)]
    greeted += [at.x_peer(lax.rem(x + d, XS)) for d in range(1, XS)]
    greeted += [at.z_peer(lax.rem(z + d, ZS)) for d in range(1, ZS)]
    greeted += [at.near(*way) for way in CORNERS + ((1, 0), (-1, 0))]
    for device in greeted:
        pl.semaphore_signal(barrier, inc=1, device_id=device, device_id_type=pl.DeviceIdType.MESH)
    params = [
        pltpu.make_async_copy(src, t[dst], t["isem"].at[i])
        for i, (src, dst) in enumerate(
            (
                (x_in, "xin"), (k3_in, "kin3"), (k4_in, "kin4"), (gain3_in, "gain3"),
                (scale_in, "scale"), (mgain_in, "mgain"), (gain4_in, "gain4"),
                (cot_in, "cot"), (res_in, "res"),
            )
        )
    ]
    weights = [
        pltpu.make_async_copy(src, t[dst], t["wsem"].at[i])
        for i, (src, dst) in enumerate(((w1_in, "w1"), (w2_in, "w2"), (wp_in, "wp")))
    ]
    for copy in params + weights:
        copy.start()
    for copy in params:
        copy.wait()
    xin, gain_three, layer_scale, merge_gain, gain_four, cot, res = (
        t[key] for key in ("xin", "gain3", "scale", "mgain", "gain4", "cot", "res")
    )

    f3, m3 = t["f3"], t["m3"]
    for i in range(8):
        line = xin[i].astype(F32)
        for h in range(2):
            for s in range(4):
                f3[pl.ds(((3 + i) * L + 3) * 8 + 4 * h + s, W, stride=8), :] = line[
                    h * W : (h + 1) * W, s * 128 : (s + 1) * 128
                ]
    taps_in(t["kin3"], t["k3"], 2)
    taps_in(t["kin4"], t["k4"], 1)
    pl.semaphore_wait(barrier, len(greeted))
    halo_i3 = Halo(at, t, "i3")
    halo_i3.start(f3)
    halo_i3.sides(f3)
    conv(f3, 8, t["k3"], False, m3)
    halo_i3.ends(f3)
    conv(f3, 8, t["k3"], False, m3, part="rest")
    for g in range(4):
        unit, inverse = unit_of(quad(m3, W, 0, 0, g))
        part = slice(g * 64, g * 64 + 64)
        t["um"][part, :] = unit
        t["im"][part, :] = jnp.broadcast_to(inverse, (64, 128))
        t["nb"][part, :] = (unit * gain_three[...]).astype(BF16)
    weights[0].wait()

    def expand(n, carry):
        lanes = pl.ds(pl.multiple_of(n * 256, 256), 256)
        upward = jnp.dot(t["nb"][...], t["w1"][:, lanes], preferred_element_type=F32)
        cumulative = 0.5 * (1.0 + lax.erf(upward * (1.0 / math.sqrt(2.0))))
        t["hb"][:, lanes] = (upward * cumulative).astype(BF16)
        t["sl"][:, lanes] = cumulative + upward * jnp.exp(-0.5 * upward * upward) * (
            1.0 / math.sqrt(2.0 * math.pi)
        )
        return carry

    lax.fori_loop(0, 8, expand, 0)
    weights[1].wait()
    t["br"][...] = jnp.dot(t["hb"][...], t["w2"][...], preferred_element_type=F32)
    for g in range(4):
        part = slice(g * 64, g * 64 + 64)
        summed = quad(f3, L, 3, 3, g) + layer_scale[...] * t["br"][part, :]
        unit, inverse = unit_of(summed)
        t["us"][part, :] = unit
        t["is"][part, :] = jnp.broadcast_to(inverse, (64, 128))
        t["pb"][:, g * 512 : (g + 1) * 512] = (unit * merge_gain[...]).astype(BF16)
    weights[2].wait()

    f4, g4, m4 = t["f4"], t["g4"], t["m4"]
    section_in = jnp.dot(t["pb"][...], t["wp"][...], preferred_element_type=F32)
    put_four(f4, section_in.astype(BF16).astype(F32))
    halo_i4 = Halo(at, t, "i4")
    halo_i4.start(f4)
    t["small_e"][...] = jnp.zeros((128, 512), F32)
    t["small_l"][...] = jnp.zeros((64, 512), F32)
    halo_i4.sides(f4)
    conv(f4, 4, t["k4"], False, m4)
    halo_i4.ends(f4)
    conv(f4, 4, t["k4"], False, m4, part="rest")
    unit_four, inverse_four = unit_of(flat_four(m4))
    cot_four = cot[...].astype(F32)
    gain_four_part = jnp.sum(cot_four * unit_four, axis=0, keepdims=True) * scale_four
    t["small_e"][112:113, :] = gain_four_part[:, 0:512]
    t["small_e"][113:114, :] = gain_four_part[:, 512:1024]
    put_four(g4, unit_back(cot_four * gain_four[...], unit_four, inverse_four))
    halo_g4 = Halo(at, t, "g4")
    halo_g4.start(g4)
    halo_g4.sides(g4)
    conv(g4, 4, t["k4"], True, m4)
    halo_g4.ends(g4)
    conv(g4, 4, t["k4"], True, m4, part="rest")
    t["fg"][...] = (res[...].astype(F32) + flat_four(m4)).astype(BF16)

    first = k == 0

    def split(index, row, even, odd, tag):
        here = slice(row, row + even.shape[0])
        t["send_" + tag][index, here, :] = jnp.where(first, odd, even).astype(BF16)
        t["own_" + tag][index, here, :] = jnp.where(first, even, odd)

    def products_a(zz, carry):
        lanes = pl.ds(pl.multiple_of(zz * 256, 256), 256)
        out = by_rows(t["pb"][:, lanes], t["fg"][...])
        for q in range(YS):
            for xx in range(XS):
                block = out[xx * 64 : (xx + 1) * 64, q * 256 : (q + 1) * 256]
                split(q * (XS * ZS) + zz * XS + xx, 0, block[:32, :128], block[:32, 128:], "a1")
                split(xx * (YS * ZS) + zz * YS + q, 0, block[32:, :128], block[32:, 128:], "a2")
        return carry

    lax.fori_loop(0, ZS, products_a, 0)
    core = {}

    def cross(tag):
        n = tuple(CHAINS).index(tag)
        core[tag] = remote(
            t["send_" + tag], t["got_" + tag], t["s1"].at[n], t["r1"].at[n], at.core_peer()
        )
        core[tag].start()

    cross("a1")
    cross("a2")
    early, late = (
        SmallSum(at, t, tag, rows, total) for (tag, rows), total in zip(SMALL, (early_o, late_o))
    )
    tap_grads(f4, g4, 4, t["a4"])
    for s in range(4):
        lanes = slice(s * 128, (s + 1) * 128)
        t["small_e"][0:49, lanes] = t["a4"][pl.ds(s, 49, stride=8), :] * scale_four
        t["small_e"][56:105, lanes] = t["a4"][pl.ds(4 + s, 49, stride=8), :] * scale_four
    early.core()

    merge_part = scale_part = jnp.zeros((1, 512), F32)
    for g in range(4):
        part = slice(g * 64, g * 64 + 64)
        unit = t["us"][part, :]
        grad_merged = by_lanes(t["fg"][...], t["wp"][g * 512 : (g + 1) * 512, :])
        merge_part = merge_part + jnp.sum(grad_merged * unit, axis=0, keepdims=True)
        grad = unit_back(grad_merged * merge_gain[...], unit, t["is"][part, 0:1])
        scale_part = scale_part + jnp.sum(grad * t["br"][part, :], axis=0, keepdims=True)
        put_quad(t["gs3"], W, 0, 0, g, grad)
        t["gb"][part, :] = (layer_scale[...] * grad).astype(BF16)
    t["small_l"][57:58, :] = scale_part * scale_three
    t["small_l"][58:59, :] = merge_part * scale_three

    def products_b(zz, carry):
        lanes = pl.ds(pl.multiple_of(zz * 256, 256), 256)
        out = by_rows(t["hb"][:, lanes], t["gb"][...])
        for q in range(YS):
            for xx in range(XS):
                block = out[xx * 64 : (xx + 1) * 64, q * 128 : (q + 1) * 128]
                split(q * (XS * ZS) + xx * ZS + zz, 0, block[:16], block[32:48], "b1")
                split(xx * (YS * ZS) + q * ZS + zz, 0, block[16:32], block[48:], "b2")
        return carry

    lax.fori_loop(0, ZS, products_b, 0)
    cross("b1")
    cross("b2")

    per2 = 32

    def second(tag):
        me, peer = (y, at.y_peer) if tag in Y_FIRST else (x, at.x_peer)
        core[tag].wait_recv()
        exchange = Exchange(
            4, me, lambda p: t["out2_" + tag].at[pl.ds(p * per2, per2)], t["in2_" + tag],
            t["s2_" + tag], t["r2_" + tag], peer,
        )
        own, got, out = t["own_" + tag], t["got_" + tag], t["out2_" + tag]
        for d, p in enumerate(exchange.others):

            def step(i, carry, p=p):
                j = p * per2 + i
                out[j] = (own[j] + got[j].astype(F32)).astype(BF16)
                return carry

            lax.fori_loop(0, per2, step, 0, unroll=4)
            exchange.copies[d].start()
        return exchange

    seconds = {"a1": second("a1"), "a2": second("a2")}
    early.over_y()

    def narrow(n, carry):
        lanes = pl.ds(pl.multiple_of(n * 256, 256), 256)
        grad_hidden = by_lanes(t["gb"][...], t["w2"][lanes, :])
        t["gu"][:, lanes] = (grad_hidden * t["sl"][:, lanes]).astype(BF16)
        return carry

    lax.fori_loop(0, 8, narrow, 0)

    seconds["b1"] = second("b1")
    seconds["b2"] = second("b2")

    grad_normed = by_lanes(t["gu"][...], t["w1"][...])
    gain_part = jnp.zeros((1, 512), F32)
    g3 = t["g3"]
    for g in range(4):
        part = slice(g * 64, g * 64 + 64)
        unit, grad = t["um"][part, :], grad_normed[part, :]
        gain_part = gain_part + jnp.sum(grad * unit, axis=0, keepdims=True)
        grad = unit_back(grad * gain_three[...], unit, t["im"][part, 0:1])
        put_quad(g3, L, 3, 3, g, grad.astype(BF16).astype(F32))
    t["small_l"][56:57, :] = gain_part * scale_three
    halo_g3 = Halo(at, t, "g3")
    halo_g3.start(g3)

    def products_e(pair, carry):
        lanes = pl.ds(pl.multiple_of(pair * 128, 128), 128)
        for q in range(YS):
            out = by_rows(t["nb"][:, lanes], t["gu"][:, q * 512 : (q + 1) * 512])
            for hz in range(2):
                for xx in range(XS):
                    rows = slice(hz * 64 + xx * 16, hz * 64 + xx * 16 + 16)
                    zz = 2 * pair + hz
                    split(
                        q * (XS * ZS) + xx * ZS + zz, 0, out[rows, 0:128], out[rows, 256:384], "c1"
                    )
                    split(
                        xx * (YS * ZS) + q * ZS + zz, 0, out[rows, 128:256], out[rows, 384:], "c2"
                    )
        return carry

    lax.fori_loop(0, ZS // 2, products_e, 0)
    cross("c1")
    cross("c2")

    axis_of = {"x": (x, XS, at.x_peer), "y": (y, YS, at.y_peer), "z": (z, ZS, at.z_peer)}

    def axes(tag):
        one, two = ("y", "x") if tag in Y_FIRST else ("x", "y")
        return (one, "z", two) if tag in Z_EARLY else (one, two, "z")

    def third(tag):
        before = seconds[tag]
        me = axis_of[axes(tag)[0]][0]
        me3, count, peer = axis_of[axes(tag)[1]]
        rest = 32 // count
        before.wait_recv()
        own, got, slots = t["own_" + tag], t["got_" + tag], t["in2_" + tag]
        out = t["out3_" + tag]
        exchange = Exchange(
            count, me3, lambda p: out.at[pl.ds(p * rest, rest)], t["in3_" + tag],
            t["s3_" + tag], t["r3_" + tag], peer,
        )

        def total_of(i):
            j = me * per2 + i
            acc = own[j] + got[j].astype(F32)
            for p in before.others:
                acc = acc + slots[p, i].astype(F32)
            return acc

        for d, p in enumerate(exchange.others):

            def step(i, carry, p=p):
                j = p * rest + i
                out[j] = total_of(j).astype(BF16)
                return carry

            lax.fori_loop(0, rest, step, 0, unroll=4)
            exchange.copies[d].start()

        def keep(i, carry):
            t["sum3_" + tag][i] = total_of(me3 * rest + i)
            return carry

        lax.fori_loop(0, rest, keep, 0, unroll=4)
        return exchange

    def fourth(tag):
        before = thirds[tag]
        before.wait_recv()
        me4, count, peer = axis_of[axes(tag)[2]]
        slots, kept, out = t["in3_" + tag], t["sum3_" + tag], t["out4_" + tag]

        def step(i, carry):
            acc = kept[i]
            for p in before.others:
                acc = acc + slots[p, i].astype(F32)
            kept[i] = acc
            out[i] = acc.astype(BF16)
            return carry

        lax.fori_loop(0, count, step, 0, unroll=4)
        exchange = Exchange(
            count, me4, lambda p: out.at[p], t["in4_" + tag],
            t["s4_" + tag], t["r4_" + tag], peer,
        )
        exchange.start()
        return exchange

    fourths = {}

    def collect(half, tags, fin):
        base = 0
        for tag in tags:
            exchange = fourths[tag]
            exchange.wait_recv()
            acc = t["sum3_" + tag][axis_of[axes(tag)[2]][0]]
            for p in exchange.others:
                acc = acc + t["in4_" + tag][p].astype(F32)
            fin[col, base : base + CHAINS[tag]] = acc.astype(BF16)
            base += CHAINS[tag]
        gather = Exchange(
            YS * KS, col, lambda p: fin.at[col], fin, t["sf" + half], t["rf" + half], at.col_peer
        )
        gather.start()
        return gather

    tap_grads(f3, g3, 8, t["a3"])
    for s in range(4):
        t["small_l"][0:49, s * 128 : (s + 1) * 128] = (
            t["a3"][pl.ds(s, 49, stride=8), :] + t["a3"][pl.ds(4 + s, 49, stride=8), :]
        ) * scale_three
    late.core()
    seconds["c1"] = second("c1")
    seconds["c2"] = second("c2")
    late.over_y()
    thirds = {"a1": third("a1"), "a2": third("a2")}
    early.over_x()
    thirds["b1"] = third("b1")
    thirds["b2"] = third("b2")
    halo_g3.sides(g3)
    conv(g3, 8, t["k3"], True, m3, t["gs3"])
    thirds["c1"] = third("c1")
    thirds["c2"] = third("c2")
    late.over_x()
    fourths["a1"] = fourth("a1")
    fourths["a2"] = fourth("a2")
    early.over_z()
    for tag in ("b1", "b2", "c1", "c2"):
        fourths[tag] = fourth(tag)
    late.over_z()
    halo_g3.ends(g3)
    conv(g3, 8, t["k3"], True, m3, part="rest")
    early.back_x()
    late.back_x()
    gather_a = collect("a", ("a1", "a2"), fin_a)
    gather_b = collect("b", ("b1", "b2", "c1", "c2"), fin_b)
    early.back_col()
    late.back_col()

    def leave(i, carry):
        for h in range(2):
            row = jnp.concatenate(
                [m3[pl.ds(i * (W * 8) + 4 * h + s, W, stride=8), :] for s in range(4)], axis=1
            )
            t["xout"][i, h * W : (h + 1) * W, :] = row.astype(BF16)
        return carry

    lax.fori_loop(0, 8, leave, 0)
    out_copy = pltpu.make_async_copy(t["xout"], input_o, t["osem"].at[0])
    out_copy.start()
    early.wait()
    gather_a.wait_recv()
    late.wait()
    gather_b.wait_recv()
    out_copy.wait()

    for tag in CHAINS:
        core[tag].wait_send()
    for tag in CHAINS:
        for stage in (seconds, thirds, fourths):
            stage[tag].wait_send()
    for exchange in (
        halo_i3, halo_i4, halo_g4, halo_g3, gather_a, gather_b, early, late,
    ):
        exchange.wait_send()


def results_kernel(
    scale_three, scale_four, input_i, fin_a, fin_b, early, late,
    input_o, k3_o, gain3_o, expand_o, project_o, scale_o, merge_o, patch_o, k4_o, gain4_o,
):
    input_o[...] = input_i[...]
    for c in range(YS * KS):
        q, kk = divmod(c, KS)
        patch_o[:, c * 128 : (c + 1) * 128] = fin_a[c].astype(F32) * scale_four
        project_o[kk * 32 : (kk + 1) * 32, q * 128 : (q + 1) * 128] = (
            fin_b[c, 0:32].astype(F32) * scale_three
        )
        for half in range(2):
            lane = c * 256 + half * 128
            expand_o[:, lane : lane + 128] = (
                fin_b[c, 32 + half * 16 : 48 + half * 16].astype(F32) * scale_three
            )
    for p in range(7):
        k3_o[p] = late[7 * p : 7 * p + 7, :]
        k4_o[p, :, 0:512] = early[7 * p : 7 * p + 7, :]
        k4_o[p, :, 512:1024] = early[56 + 7 * p : 63 + 7 * p, :]
    gain3_o[...] = late[56:57, :]
    scale_o[...] = late[57:58, :]
    merge_o[...] = late[58:59, :]
    gain4_o[:, 0:512] = early[112:113, :]
    gain4_o[:, 512:1024] = early[113:114, :]


def body(
    block_input,
    kernel_three,
    gain_three,
    expand_weight,
    project_weight,
    layer_scale,
    merge_gain,
    patch_weight,
    kernel_four,
    gain_four,
    normed_cotangent,
    residual_cotangent,
):
    devices = lax.axis_size("row") * lax.axis_size("col")
    scale_three = 1.0 / math.sqrt(256 * devices)
    scale_four = 1.0 / math.sqrt(64 * devices)
    table = scratch_table()
    whole = pl.BlockSpec(memory_space=pltpu.VMEM)
    away = pl.BlockSpec(memory_space=pl.ANY)
    flat = lambda v: v.reshape(1, -1)
    moved = pl.pallas_call(
        functools.partial(kernel, scale_three, scale_four, tuple(table)),
        out_shape=(
            jax.ShapeDtypeStruct((8, 32, 512), BF16),
            jax.ShapeDtypeStruct((8, 64, 128), BF16),
            jax.ShapeDtypeStruct((8, 64, 128), BF16),
            jax.ShapeDtypeStruct((128, 512), F32),
            jax.ShapeDtypeStruct((64, 512), F32),
        ),
        in_specs=[away] * 12,
        out_specs=(away,) + (whole,) * 4,
        scratch_shapes=list(table.values()),
        compiler_params=pltpu.CompilerParams(
            collective_id=0, has_side_effects=True, vmem_limit_bytes=60 << 20
        ),
        name="block_backward",
    )(
        block_input.reshape(8, 32, 512),
        kernel_three,
        flat(gain_three),
        expand_weight,
        project_weight,
        flat(layer_scale),
        flat(merge_gain),
        patch_weight,
        kernel_four,
        flat(gain_four),
        normed_cotangent.reshape(64, 1024),
        residual_cotangent.reshape(64, 1024),
    )
    shapes = (
        (8, 32, 512), (7, 7, 512), (1, 512), (16, 2048), (64, 512),
        (1, 512), (1, 512), (64, 1024), (7, 7, 1024), (1, 1024),
    )
    outs = pl.pallas_call(
        functools.partial(results_kernel, scale_three, scale_four),
        out_shape=tuple(
            jax.ShapeDtypeStruct(shape, F32 if n else BF16) for n, shape in enumerate(shapes)
        ),
        in_specs=[whole] * 5,
        out_specs=(whole,) * 10,
        compiler_params=pltpu.CompilerParams(vmem_limit_bytes=16 << 20),
        name="results",
    )(*moved)
    outs = list(outs)
    outs[0] = outs[0].reshape(1, 8, 32, 512)
    for n in (2, 5, 6, 9):
        outs[n] = outs[n].reshape(-1)
    return tuple(outs)


def solution(mesh):
    pixels = P(None, "row", "col", None)
    return jax.shard_map(
        body,
        mesh=mesh,
        in_specs=(pixels,) + (P(),) * 9 + (pixels, pixels),
        out_specs=(pixels, P(), P(), P("row", None), P("row", None), P(), P(), P("row", None), P(), P()),
        check_vma=False,
    )
```

```python
import functools
import math

import jax
import jax.numpy as jnp
from jax import lax
from jax.experimental import pallas as pl
from jax.experimental.pallas import tpu as pltpu
from jax.sharding import PartitionSpec as P

EPSILON = 1e-06
F32 = jnp.float32
BF16 = jnp.bfloat16
XS, YS, ZS, KS = 4, 4, 8, 2


class Place:
    def __init__(self):
        row, col = lax.axis_index("row"), lax.axis_index("col")
        self.row, self.col = row, col
        self.x, self.z = lax.rem(row, XS), lax.div(row, XS)
        self.k, self.y = lax.rem(col, KS), lax.div(col, KS)

    def near(self, down, right):
        rows, cols = XS * ZS, YS * KS
        return {
            "row": lax.rem(self.row + (down + rows), rows),
            "col": lax.rem(self.col + (right + cols), cols),
        }

    def core_peer(self):
        return {"row": self.row, "col": self.y * KS + (1 - self.k)}

    def y_peer(self, y):
        return {"row": self.row, "col": y * KS + self.k}

    def x_peer(self, x):
        return {"row": self.z * XS + x, "col": self.col}

    def z_peer(self, z):
        return {"row": z * XS + self.x, "col": self.col}

    def col_peer(self, col):
        return {"row": self.row, "col": col}


def remote(src, dst, send, recv, device):
    return pltpu.make_async_remote_copy(
        src_ref=src,
        dst_ref=dst,
        send_sem=send,
        recv_sem=recv,
        device_id=device,
        device_id_type=pl.DeviceIdType.MESH,
    )


class Exchange:
    def __init__(self, count, me, piece, slots, send, recv, peer):
        far_first = sorted(range(1, count), key=lambda d: -min(d, count - d))
        self.others = [lax.rem(me + d, count) for d in far_first]
        self.copies = [
            remote(piece(p), slots.at[me], send.at[d], recv.at[me], peer(p))
            for d, p in enumerate(self.others)
        ]
        self.arrivals = [
            remote(piece(p), slots.at[p], send.at[d], recv.at[p], peer(p))
            for d, p in enumerate(self.others)
        ]

    def start(self):
        for copy in self.copies:
            copy.start()

    def wait_recv(self):
        for copy in self.arrivals:
            copy.wait_recv()

    def wait_send(self):
        for copy in self.copies:
            copy.wait_send()


W = 16
L = W + 6
CORNERS = ((1, 1), (1, -1), (-1, 1), (-1, -1))
HALOS = ("i3", "i4", "g4", "g3")
CHAINS = {"a1": 32, "a2": 32, "b1": 16, "b2": 16, "c1": 16, "c2": 16}
Y_FIRST = ("a1", "b1", "c1")
Z_EARLY = ("a1", "a2")
SMALL = (("e", 16), ("l", 8))


def halo_rows(name):
    return 8 if name.endswith("3") else 4


def scratch_table():
    vm, dma = pltpu.VMEM, pltpu.SemaphoreType.DMA
    packed = lambda pixels: vm((pixels * 8, 128), F32)
    table = {
        "w1": vm((512, 2048), BF16),
        "w2": vm((2048, 512), BF16),
        "wp": vm((2048, 1024), BF16),
        "wsem": dma((3,)),
        "f3": packed(14 * L), "g3": packed(14 * L), "m3": packed(8 * W), "gs3": packed(8 * W),
        "f4": packed(10 * L), "g4": packed(10 * L), "m4": packed(4 * W),
        "k3": packed(49), "k4": packed(49), "a3": packed(49), "a4": packed(49),
        "um": vm((256, 512), F32), "im": vm((256, 128), F32), "nb": vm((256, 512), BF16),
        "hb": vm((256, 2048), BF16), "sl": vm((256, 2048), F32), "br": vm((256, 512), F32),
        "us": vm((256, 512), F32), "is": vm((256, 128), F32), "pb": vm((64, 2048), BF16),
        "fg": vm((64, 1024), BF16), "gb": vm((256, 512), BF16),
        "gu": vm((256, 2048), BF16),
    }
    for name in HALOS:
        rows = halo_rows(name)
        table["c_" + name] = vm((rows, W, 8, 128), BF16)
        table["v_" + name] = vm((2, 3, W, 8, 128), BF16)
        table["h_" + name] = vm((2, rows, 3, 8, 128), BF16)
        table["d_" + name] = vm((4, 3, 3, 8, 128), BF16)
        table["s_" + name] = dma((8,))
        table["r_" + name] = dma((8,))
    for tag, rows in SMALL:
        table["small_" + tag] = vm((8 * rows, 512), F32)
        for name, shape in (
            ("got_", (YS * rows, 512)), ("acc_", (YS, rows, 512)), ("iny_", (YS, rows, 512)),
            ("xp_", (XS, rows, 128)), ("inx_", (XS, rows, 128)), ("z_", (ZS, rows, 128)),
            ("fin_", (XS, rows, 128)),
        ):
            table["sm" + name + tag] = vm(shape, F32)
        for name, count in (("k", 1), ("y", YS), ("x", XS), ("z", ZS), ("g", XS), ("c", YS * KS)):
            table["sm_s" + name + tag] = dma((count,))
            table["sm_r" + name + tag] = dma((count,))
    pieces = YS * XS * ZS
    for t, deep in CHAINS.items():
        table["send_" + t] = vm((pieces, deep, 128), BF16)
        table["got_" + t] = vm((pieces, deep, 128), BF16)
        table["own_" + t] = vm((pieces, deep, 128), F32)
        table["out2_" + t] = vm((pieces, deep, 128), BF16)
        table["in2_" + t] = vm((4, 32, deep, 128), BF16)
        table["out3_" + t] = vm((32, deep, 128), BF16)
        third = ZS if t in Z_EARLY else 4
        table["in3_" + t] = vm((third, 32 // third, deep, 128), BF16)
        table["sum3_" + t] = vm((32 // third, deep, 128), F32)
        table["out4_" + t] = vm((32 // third, deep, 128), BF16)
        table["in4_" + t] = vm((32 // third, deep, 128), BF16)
        for stage, count in ((2, 4), (3, third), (4, 32 // third)):
            table["s%d_%s" % (stage, t)] = dma((count,))
            table["r%d_%s" % (stage, t)] = dma((count,))
    table.update(
        xin=vm((8, 32, 512), BF16), kin3=vm((7, 7, 512), F32), kin4=vm((7, 7, 1024), F32),
        gain3=vm((1, 512), F32), scale=vm((1, 512), F32), mgain=vm((1, 512), F32),
        gain4=vm((1, 1024), F32), cot=vm((64, 1024), BF16), res=vm((64, 1024), BF16),
        isem=dma((9,)), osem=dma((1,)), xout=vm((8, 32, 512), BF16),
        s1=dma((6,)), r1=dma((6,)),
        sfa=dma((YS * KS,)), rfa=dma((YS * KS,)), sfb=dma((YS * KS,)), rfb=dma((YS * KS,)),
    )
    return table


def pixels_at(ref, start, count):
    return ref[pl.ds(pl.multiple_of(start * 8, 8), count * 8), :].reshape(count, 8, 128)


def put_pixels(ref, start, value):
    count = value.shape[0]
    ref[pl.ds(pl.multiple_of(start * 8, 8), count * 8), :] = value.reshape(count * 8, 128)


def taps_in(weights, ref, groups):
    lanes = 8 // groups
    for p in range(7):
        line = weights[p]
        for g in range(groups):
            for s in range(lanes):
                ref[pl.ds(p * 56 + g * lanes + s, 7, stride=8), :] = line[
                    :, s * 128 : (s + 1) * 128
                ]


def quad(ref, length, row, column, g):
    dy, dx = divmod(g, 2)
    rows = []
    for yy in range(4):
        for h in range(2):
            start = ((row + 2 * yy + dy) * length + column + dx) * 8 + 4 * h
            rows.append(
                jnp.concatenate([ref[pl.ds(start + s, 8, stride=16), :] for s in range(4)], axis=1)
            )
    return jnp.concatenate(rows, axis=0)


def put_quad(ref, length, row, column, g, value):
    dy, dx = divmod(g, 2)
    for yy in range(4):
        for h in range(2):
            start = ((row + 2 * yy + dy) * length + column + dx) * 8 + 4 * h
            top = yy * 16 + h * 8
            for s in range(4):
                ref[pl.ds(start + s, 8, stride=16), :] = value[
                    top : top + 8, s * 128 : (s + 1) * 128
                ]


def flat_four(ref):
    return jnp.concatenate([ref[pl.ds(s, 64, stride=8), :] for s in range(8)], axis=1)


def put_four(ref, value):
    for i in range(4):
        for s in range(8):
            ref[pl.ds(((3 + i) * L + 3) * 8 + s, W, stride=8), :] = value[
                i * W : (i + 1) * W, s * 128 : (s + 1) * 128
            ]


def conv(framed, rows, taps, flip, out, base=None, part="own"):
    def gather_rows(i, low, high, acc):
        def over_p(p, acc):
            line = pixels_at(framed, (i + p) * L, L)
            for q in range(7):
                tap = (6 - p) * 7 + (6 - q) if flip else p * 7 + q
                acc = acc + line[q : q + W] * taps[pl.ds(pl.multiple_of(tap * 8, 8), 8), :]
            return acc

        return lax.fori_loop(low, high, over_p, acc)

    def own(i, carry):
        acc = jnp.zeros((W, 8, 128), F32) if base is None else pixels_at(base, i * W, W)
        acc = gather_rows(i, jnp.maximum(3 - i, 0), jnp.minimum(rows + 3 - i, 7), acc)
        put_pixels(out, i * W, acc)
        return carry

    def above(i, carry):
        put_pixels(out, i * W, gather_rows(i, 0, 3 - i, pixels_at(out, i * W, W)))
        return carry

    def below(i, carry):
        put_pixels(out, i * W, gather_rows(i, rows + 3 - i, 7, pixels_at(out, i * W, W)))
        return carry

    if part == "own":
        lax.fori_loop(0, rows, own, 0)
    else:
        lax.fori_loop(0, 3, above, 0)
        lax.fori_loop(rows - 3, rows, below, 0)


def tap_grads(framed, grads, rows, out):
    def over_p(p, carry):
        def over_rows(i, accs):
            line = pixels_at(framed, (i + p) * L, L)
            grad = pixels_at(grads, (i + 3) * L + 3, W)
            return tuple(acc + jnp.sum(line[q : q + W] * grad, axis=0) for q, acc in enumerate(accs))

        accs = lax.fori_loop(0, rows, over_rows, (jnp.zeros((8, 128), F32),) * 7)
        for q in range(7):
            put_pixels(out, p * 7 + q, accs[q][None])
        return carry

    lax.fori_loop(0, 7, over_p, 0)


class Halo:
    def __init__(self, at, t, name):
        self.rows = rows = halo_rows(name)
        self.at, self.t, self.name = at, t, name
        c, v, h, d = (t[key + name] for key in ("c_", "v_", "h_", "d_"))
        s, r = t["s_" + name], t["r_" + name]
        three = lambda way, size: pl.ds(size - 3, 3) if way > 0 else pl.ds(0, 3)
        self.copies = []
        for n, way in enumerate((1, -1)):
            self.copies.append(
                remote(c.at[three(way, rows)], v.at[n], s.at[n], r.at[n], at.near(way, 0))
            )
            self.copies.append(
                remote(c.at[:, three(way, W)], h.at[n], s.at[2 + n], r.at[2 + n], at.near(0, way))
            )
        for n, (down, right) in enumerate(CORNERS):
            self.copies.append(
                remote(
                    c.at[three(down, rows), three(right, W)], d.at[n], s.at[4 + n], r.at[4 + n],
                    at.near(down, right),
                )
            )

    def start(self, framed):
        c = self.t["c_" + self.name]

        def step(i, carry):
            c[i] = pixels_at(framed, (i + 3) * L + 3, W).astype(BF16)
            return carry

        lax.fori_loop(0, self.rows, step, 0)
        for copy in self.copies:
            copy.start()

    def wait_send(self):
        for copy in self.copies:
            copy.wait_send()

    def fill_sides(self, framed, lines):
        at, rows = self.at, self.rows
        h, d = self.t["h_" + self.name], self.t["d_" + self.name]
        one = lambda ok: jnp.where(ok, 1.0, 0.0).astype(F32)
        up, down = one(at.row > 0), one(at.row < XS * ZS - 1)
        left, right = one(at.col > 0), one(at.col < YS * KS - 1)
        for n, (side, start) in enumerate(((left, 0), (right, W + 3))):
            for i in lines:
                if i < 3:
                    value = d[n, i].astype(F32) * (side * up)
                elif i < rows + 3:
                    value = h[n, i - 3].astype(F32) * side
                else:
                    value = d[2 + n, i - rows - 3].astype(F32) * (side * down)
                if rows == 8:
                    inner = pixels_at(framed, i * L + (W if n == 0 else 3), 3)
                    first, second = (value, inner) if n == 0 else (inner, value)
                    value = jnp.concatenate([first[:, 4:8], second[:, 0:4]], axis=1)
                put_pixels(framed, i * L + start, value)

    def sides(self, framed):
        for copy in self.copies[1:4:2]:
            copy.wait_recv()
        self.fill_sides(framed, range(3, self.rows + 3))

    def ends(self, framed):
        for copy in self.copies[0:4:2] + self.copies[4:]:
            copy.wait_recv()
        at, rows = self.at, self.rows
        v = self.t["v_" + self.name]
        one = lambda ok: jnp.where(ok, 1.0, 0.0).astype(F32)
        up, down = one(at.row > 0), one(at.row < XS * ZS - 1)
        for n, (ok, first) in enumerate(((up, 0), (down, rows + 3))):
            for i in range(3):
                put_pixels(framed, (first + i) * L + 3, v[n, i].astype(F32) * ok)
        self.fill_sides(framed, [0, 1, 2, rows + 3, rows + 4, rows + 5])


class SmallSum:
    def __init__(self, at, t, tag, rows, total):
        self.at, self.t, self.tag, self.rows, self.total = at, t, tag, rows, total
        self.sends = []

    def ref(self, name):
        return self.t["sm" + name + self.tag]

    def sems(self, name):
        return self.ref("_s" + name), self.ref("_r" + name)

    def group(self, index, count=1):
        return pl.ds(pl.multiple_of(index * self.rows, 8), count * self.rows)

    def exchange(self, count, me, piece, slots, name, peer):
        result = Exchange(count, me, piece, slots, *self.sems(name), peer)
        result.start()
        self.sends.append(result)
        return result

    def core(self):
        at, got, (send, recv) = self.at, self.ref("got_"), self.sems("k")
        small = self.t["small_" + self.tag]
        self.crossing = [
            remote(
                small.at[self.group((1 - at.k) * YS, YS)], got, send.at[0], recv.at[0],
                at.core_peer(),
            )
        ]
        self.crossing[0].start()

    def over_y(self):
        at, acc, got = self.at, self.ref("acc_"), self.ref("got_")
        small = self.t["small_" + self.tag]
        self.crossing[0].wait_recv()
        for q in range(YS):
            part = slice(q * self.rows, (q + 1) * self.rows)
            acc[q] = small[self.group(at.k * YS + q), :] + got[part, :]
        self.y = self.exchange(YS, at.y, lambda p: acc.at[p], self.ref("iny_"), "y", at.y_peer)

    def over_x(self):
        at, pieces = self.at, self.ref("xp_")
        self.y.wait_recv()
        total = self.ref("acc_")[at.y]
        for p in self.y.others:
            total = total + self.ref("iny_")[p]
        for xx in range(XS):
            pieces[xx] = total[:, xx * 128 : (xx + 1) * 128]
        self.x = self.exchange(XS, at.x, lambda p: pieces.at[p], self.ref("inx_"), "x", at.x_peer)

    def over_z(self):
        at, slots = self.at, self.ref("z_")
        self.x.wait_recv()
        total = self.ref("xp_")[at.x]
        for p in self.x.others:
            total = total + self.ref("inx_")[p]
        slots[at.z] = total
        self.z = self.exchange(ZS, at.z, lambda p: slots.at[at.z], slots, "z", at.z_peer)

    def back_x(self):
        at, slots = self.at, self.ref("fin_")
        self.z.wait_recv()
        total = self.ref("z_")[0]
        for p in range(1, ZS):
            total = total + self.ref("z_")[p]
        slots[at.x] = total
        self.g = self.exchange(XS, at.x, lambda p: slots.at[at.x], slots, "g", at.x_peer)

    def back_col(self):
        at, total = self.at, self.total
        self.g.wait_recv()
        number = lambda c: lax.rem(c, KS) * YS + lax.div(c, KS)
        mine = self.group(number(at.col))
        total[mine, :] = jnp.concatenate([self.ref("fin_")[q] for q in range(XS)], axis=1)
        send, recv = self.sems("c")
        self.last, self.arrivals = [], []
        for d in range(1, YS * KS):
            c = lax.rem(at.col + d, YS * KS)
            self.last.append(
                remote(
                    total.at[mine], total.at[mine], send.at[d], recv.at[number(at.col)],
                    at.col_peer(c),
                )
            )
            self.arrivals.append(
                remote(
                    total.at[mine], total.at[self.group(number(c))], send.at[d],
                    recv.at[number(c)], at.col_peer(c),
                )
            )
        for copy in self.last:
            copy.start()

    def wait(self):
        for copy in self.arrivals:
            copy.wait_recv()

    def wait_send(self):
        for copy in self.crossing + self.last:
            copy.wait_send()
        for exchange in self.sends:
            exchange.wait_send()


def unit_of(values):
    mean_value = jnp.mean(values, axis=-1, keepdims=True)
    square = jnp.mean(values * values, axis=-1, keepdims=True)
    inverse = lax.rsqrt(square - mean_value * mean_value + EPSILON)
    return (values - mean_value) * inverse, inverse


def unit_back(grads, unit_values, inverse):
    return (
        grads
        - jnp.mean(grads, axis=-1, keepdims=True)
        - unit_values * jnp.mean(grads * unit_values, axis=-1, keepdims=True)
    ) * inverse


def by_rows(left, right):
    return lax.dot_general(left, right, (((0,), (0,)), ((), ())), preferred_element_type=F32)


def by_lanes(left, right):
    return lax.dot_general(left, right, (((1,), (1,)), ((), ())), preferred_element_type=F32)


def kernel(
    scale_three, scale_four, names,
    x_in, k3_in, gain3_in, w1_in, w2_in, scale_in, mgain_in, wp_in, k4_in, gain4_in, cot_in, res_in,
    input_o, fin_a, fin_b, early_o, late_o,
    *scratch,
):
    t = dict(zip(names, scratch))
    at = Place()
    x, y, z, k, col = at.x, at.y, at.z, at.k, at.col
    barrier = pltpu.get_barrier_semaphore()
    greeted = [at.col_peer(lax.rem(col + d, YS * KS)) for d in range(1, YS * KS)]
    greeted += [at.x_peer(lax.rem(x + d, XS)) for d in range(1, XS)]
    greeted += [at.z_peer(lax.rem(z + d, ZS)) for d in range(1, ZS)]
    greeted += [at.near(*way) for way in CORNERS + ((1, 0), (-1, 0))]
    for device in greeted:
        pl.semaphore_signal(barrier, inc=1, device_id=device, device_id_type=pl.DeviceIdType.MESH)
    params = [
        pltpu.make_async_copy(src, t[dst], t["isem"].at[i])
        for i, (src, dst) in enumerate(
            (
                (x_in, "xin"), (k3_in, "kin3"), (k4_in, "kin4"), (gain3_in, "gain3"),
                (scale_in, "scale"), (mgain_in, "mgain"), (gain4_in, "gain4"),
                (cot_in, "cot"), (res_in, "res"),
            )
        )
    ]
    weights = [
        pltpu.make_async_copy(src, t[dst], t["wsem"].at[i])
        for i, (src, dst) in enumerate(((w1_in, "w1"), (w2_in, "w2"), (wp_in, "wp")))
    ]
    for copy in params + weights:
        copy.start()
    for copy in params:
        copy.wait()
    xin, gain_three, layer_scale, merge_gain, gain_four, cot, res = (
        t[key] for key in ("xin", "gain3", "scale", "mgain", "gain4", "cot", "res")
    )

    f3, m3 = t["f3"], t["m3"]
    for i in range(8):
        line = xin[i].astype(F32)
        for h in range(2):
            for s in range(4):
                f3[pl.ds(((3 + i) * L + 3) * 8 + 4 * h + s, W, stride=8), :] = line[
                    h * W : (h + 1) * W, s * 128 : (s + 1) * 128
                ]
    taps_in(t["kin3"], t["k3"], 2)
    taps_in(t["kin4"], t["k4"], 1)
    pl.semaphore_wait(barrier, len(greeted))
    halo_i3 = Halo(at, t, "i3")
    halo_i3.start(f3)
    halo_i3.sides(f3)
    conv(f3, 8, t["k3"], False, m3)
    halo_i3.ends(f3)
    conv(f3, 8, t["k3"], False, m3, part="rest")
    for g in range(4):
        unit, inverse = unit_of(quad(m3, W, 0, 0, g))
        part = slice(g * 64, g * 64 + 64)
        t["um"][part, :] = unit
        t["im"][part, :] = jnp.broadcast_to(inverse, (64, 128))
        t["nb"][part, :] = (unit * gain_three[...]).astype(BF16)
    weights[0].wait()

    def expand(n, carry):
        lanes = pl.ds(pl.multiple_of(n * 256, 256), 256)
        upward = jnp.dot(t["nb"][...], t["w1"][:, lanes], preferred_element_type=F32)
        cumulative = 0.5 * (1.0 + lax.erf(upward * (1.0 / math.sqrt(2.0))))
        t["hb"][:, lanes] = (upward * cumulative).astype(BF16)
        t["sl"][:, lanes] = cumulative + upward * jnp.exp(-0.5 * upward * upward) * (
            1.0 / math.sqrt(2.0 * math.pi)
        )
        return carry

    lax.fori_loop(0, 8, expand, 0)
    weights[1].wait()
    t["br"][...] = jnp.dot(t["hb"][...], t["w2"][...], preferred_element_type=F32)
    for g in range(4):
        part = slice(g * 64, g * 64 + 64)
        summed = quad(f3, L, 3, 3, g) + layer_scale[...] * t["br"][part, :]
        unit, inverse = unit_of(summed)
        t["us"][part, :] = unit
        t["is"][part, :] = jnp.broadcast_to(inverse, (64, 128))
        t["pb"][:, g * 512 : (g + 1) * 512] = (unit * merge_gain[...]).astype(BF16)
    weights[2].wait()

    f4, g4, m4 = t["f4"], t["g4"], t["m4"]
    section_in = jnp.dot(t["pb"][...], t["wp"][...], preferred_element_type=F32)
    put_four(f4, section_in.astype(BF16).astype(F32))
    halo_i4 = Halo(at, t, "i4")
    halo_i4.start(f4)
    t["small_e"][...] = jnp.zeros((128, 512), F32)
    t["small_l"][...] = jnp.zeros((64, 512), F32)
    halo_i4.sides(f4)
    conv(f4, 4, t["k4"], False, m4)
    halo_i4.ends(f4)
    conv(f4, 4, t["k4"], False, m4, part="rest")
    unit_four, inverse_four = unit_of(flat_four(m4))
    cot_four = cot[...].astype(F32)
    gain_four_part = jnp.sum(cot_four * unit_four, axis=0, keepdims=True) * scale_four
    t["small_e"][112:113, :] = gain_four_part[:, 0:512]
    t["small_e"][113:114, :] = gain_four_part[:, 512:1024]
    put_four(g4, unit_back(cot_four * gain_four[...], unit_four, inverse_four))
    halo_g4 = Halo(at, t, "g4")
    halo_g4.start(g4)
    tap_grads(f4, g4, 4, t["a4"])
    for s in range(4):
        lanes = slice(s * 128, (s + 1) * 128)
        t["small_e"][0:49, lanes] = t["a4"][pl.ds(s, 49, stride=8), :] * scale_four
        t["small_e"][56:105, lanes] = t["a4"][pl.ds(4 + s, 49, stride=8), :] * scale_four
    halo_g4.sides(g4)
    conv(g4, 4, t["k4"], True, m4)
    halo_g4.ends(g4)
    conv(g4, 4, t["k4"], True, m4, part="rest")
    t["fg"][...] = (res[...].astype(F32) + flat_four(m4)).astype(BF16)

    first = k == 0

    def split(index, row, even, odd, tag):
        here = slice(row, row + even.shape[0])
        t["send_" + tag][index, here, :] = jnp.where(first, odd, even).astype(BF16)
        t["own_" + tag][index, here, :] = jnp.where(first, even, odd)

    def products_a(zz, carry):
        lanes = pl.ds(pl.multiple_of(zz * 256, 256), 256)
        out = by_rows(t["pb"][:, lanes], t["fg"][...])
        for q in range(YS):
            for xx in range(XS):
                block = out[xx * 64 : (xx + 1) * 64, q * 256 : (q + 1) * 256]
                split(q * (XS * ZS) + zz * XS + xx, 0, block[:32, :128], block[:32, 128:], "a1")
                split(xx * (YS * ZS) + zz * YS + q, 0, block[32:, :128], block[32:, 128:], "a2")
        return carry

    lax.fori_loop(0, ZS, products_a, 0)
    core = {}

    def cross(tag):
        n = tuple(CHAINS).index(tag)
        core[tag] = remote(
            t["send_" + tag], t["got_" + tag], t["s1"].at[n], t["r1"].at[n], at.core_peer()
        )
        core[tag].start()

    cross("a1")
    cross("a2")
    early, late = (
        SmallSum(at, t, tag, rows, total) for (tag, rows), total in zip(SMALL, (early_o, late_o))
    )
    early.core()

    merge_part = scale_part = jnp.zeros((1, 512), F32)
    for g in range(4):
        part = slice(g * 64, g * 64 + 64)
        unit = t["us"][part, :]
        grad_merged = by_lanes(t["fg"][...], t["wp"][g * 512 : (g + 1) * 512, :])
        merge_part = merge_part + jnp.sum(grad_merged * unit, axis=0, keepdims=True)
        grad = unit_back(grad_merged * merge_gain[...], unit, t["is"][part, 0:1])
        scale_part = scale_part + jnp.sum(grad * t["br"][part, :], axis=0, keepdims=True)
        put_quad(t["gs3"], W, 0, 0, g, grad)
        t["gb"][part, :] = (layer_scale[...] * grad).astype(BF16)
    t["small_l"][57:58, :] = scale_part * scale_three
    t["small_l"][58:59, :] = merge_part * scale_three

    def products_b(zz, carry):
        lanes = pl.ds(pl.multiple_of(zz * 256, 256), 256)
        out = by_rows(t["hb"][:, lanes], t["gb"][...])
        for q in range(YS):
            for xx in range(XS):
                block = out[xx * 64 : (xx + 1) * 64, q * 128 : (q + 1) * 128]
                split(q * (XS * ZS) + xx * ZS + zz, 0, block[:16], block[32:48], "b1")
                split(xx * (YS * ZS) + q * ZS + zz, 0, block[16:32], block[48:], "b2")
        return carry

    lax.fori_loop(0, ZS, products_b, 0)
    cross("b1")
    cross("b2")

    per2 = 32

    def second(tag):
        me, peer = (y, at.y_peer) if tag in Y_FIRST else (x, at.x_peer)
        core[tag].wait_recv()
        exchange = Exchange(
            4, me, lambda p: t["out2_" + tag].at[pl.ds(p * per2, per2)], t["in2_" + tag],
            t["s2_" + tag], t["r2_" + tag], peer,
        )
        own, got, out = t["own_" + tag], t["got_" + tag], t["out2_" + tag]
        for d, p in enumerate(exchange.others):

            def step(i, carry, p=p):
                j = p * per2 + i
                out[j] = (own[j] + got[j].astype(F32)).astype(BF16)
                return carry

            lax.fori_loop(0, per2, step, 0, unroll=4)
            exchange.copies[d].start()
        return exchange

    seconds = {"a1": second("a1"), "a2": second("a2")}
    early.over_y()

    def narrow(n, carry):
        lanes = pl.ds(pl.multiple_of(n * 256, 256), 256)
        grad_hidden = by_lanes(t["gb"][...], t["w2"][lanes, :])
        t["gu"][:, lanes] = (grad_hidden * t["sl"][:, lanes]).astype(BF16)
        return carry

    lax.fori_loop(0, 8, narrow, 0)

    seconds["b1"] = second("b1")
    seconds["b2"] = second("b2")

    grad_normed = by_lanes(t["gu"][...], t["w1"][...])
    gain_part = jnp.zeros((1, 512), F32)
    g3 = t["g3"]
    for g in range(4):
        part = slice(g * 64, g * 64 + 64)
        unit, grad = t["um"][part, :], grad_normed[part, :]
        gain_part = gain_part + jnp.sum(grad * unit, axis=0, keepdims=True)
        grad = unit_back(grad * gain_three[...], unit, t["im"][part, 0:1])
        put_quad(g3, L, 3, 3, g, grad.astype(BF16).astype(F32))
    t["small_l"][56:57, :] = gain_part * scale_three
    halo_g3 = Halo(at, t, "g3")
    halo_g3.start(g3)

    def products_e(pair, carry):
        lanes = pl.ds(pl.multiple_of(pair * 128, 128), 128)
        for q in range(YS):
            out = by_rows(t["nb"][:, lanes], t["gu"][:, q * 512 : (q + 1) * 512])
            for hz in range(2):
                for xx in range(XS):
                    rows = slice(hz * 64 + xx * 16, hz * 64 + xx * 16 + 16)
                    zz = 2 * pair + hz
                    split(
                        q * (XS * ZS) + xx * ZS + zz, 0, out[rows, 0:128], out[rows, 256:384], "c1"
                    )
                    split(
                        xx * (YS * ZS) + q * ZS + zz, 0, out[rows, 128:256], out[rows, 384:], "c2"
                    )
        return carry

    lax.fori_loop(0, ZS // 2, products_e, 0)
    cross("c1")
    cross("c2")

    axis_of = {"x": (x, XS, at.x_peer), "y": (y, YS, at.y_peer), "z": (z, ZS, at.z_peer)}

    def axes(tag):
        one, two = ("y", "x") if tag in Y_FIRST else ("x", "y")
        return (one, "z", two) if tag in Z_EARLY else (one, two, "z")

    def third(tag):
        before = seconds[tag]
        me = axis_of[axes(tag)[0]][0]
        me3, count, peer = axis_of[axes(tag)[1]]
        rest = 32 // count
        before.wait_recv()
        own, got, slots = t["own_" + tag], t["got_" + tag], t["in2_" + tag]
        out = t["out3_" + tag]
        exchange = Exchange(
            count, me3, lambda p: out.at[pl.ds(p * rest, rest)], t["in3_" + tag],
            t["s3_" + tag], t["r3_" + tag], peer,
        )

        def total_of(i):
            j = me * per2 + i
            acc = own[j] + got[j].astype(F32)
            for p in before.others:
                acc = acc + slots[p, i].astype(F32)
            return acc

        for d, p in enumerate(exchange.others):

            def step(i, carry, p=p):
                j = p * rest + i
                out[j] = total_of(j).astype(BF16)
                return carry

            lax.fori_loop(0, rest, step, 0, unroll=4)
            exchange.copies[d].start()

        def keep(i, carry):
            t["sum3_" + tag][i] = total_of(me3 * rest + i)
            return carry

        lax.fori_loop(0, rest, keep, 0, unroll=4)
        return exchange

    def fourth(tag):
        before = thirds[tag]
        before.wait_recv()
        me4, count, peer = axis_of[axes(tag)[2]]
        slots, kept, out = t["in3_" + tag], t["sum3_" + tag], t["out4_" + tag]

        def step(i, carry):
            acc = kept[i]
            for p in before.others:
                acc = acc + slots[p, i].astype(F32)
            kept[i] = acc
            out[i] = acc.astype(BF16)
            return carry

        lax.fori_loop(0, count, step, 0, unroll=4)
        exchange = Exchange(
            count, me4, lambda p: out.at[p], t["in4_" + tag],
            t["s4_" + tag], t["r4_" + tag], peer,
        )
        exchange.start()
        return exchange

    fourths = {}

    def collect(half, tags, fin):
        base = 0
        for tag in tags:
            exchange = fourths[tag]
            exchange.wait_recv()
            acc = t["sum3_" + tag][axis_of[axes(tag)[2]][0]]
            for p in exchange.others:
                acc = acc + t["in4_" + tag][p].astype(F32)
            fin[col, base : base + CHAINS[tag]] = acc.astype(BF16)
            base += CHAINS[tag]
        gather = Exchange(
            YS * KS, col, lambda p: fin.at[col], fin, t["sf" + half], t["rf" + half], at.col_peer
        )
        gather.start()
        return gather

    tap_grads(f3, g3, 8, t["a3"])
    for s in range(4):
        t["small_l"][0:49, s * 128 : (s + 1) * 128] = (
            t["a3"][pl.ds(s, 49, stride=8), :] + t["a3"][pl.ds(4 + s, 49, stride=8), :]
        ) * scale_three
    late.core()
    seconds["c1"] = second("c1")
    seconds["c2"] = second("c2")
    late.over_y()
    thirds = {"a1": third("a1"), "a2": third("a2")}
    early.over_x()
    thirds["b1"] = third("b1")
    thirds["b2"] = third("b2")
    halo_g3.sides(g3)
    conv(g3, 8, t["k3"], True, m3, t["gs3"])
    thirds["c1"] = third("c1")
    thirds["c2"] = third("c2")
    late.over_x()
    fourths["a1"] = fourth("a1")
    fourths["a2"] = fourth("a2")
    early.over_z()
    for tag in ("b1", "b2", "c1", "c2"):
        fourths[tag] = fourth(tag)
    late.over_z()
    halo_g3.ends(g3)
    conv(g3, 8, t["k3"], True, m3, part="rest")
    early.back_x()
    late.back_x()
    gather_a = collect("a", ("a1", "a2"), fin_a)
    gather_b = collect("b", ("b1", "b2", "c1", "c2"), fin_b)
    early.back_col()
    late.back_col()

    def leave(i, carry):
        for h in range(2):
            row = jnp.concatenate(
                [m3[pl.ds(i * (W * 8) + 4 * h + s, W, stride=8), :] for s in range(4)], axis=1
            )
            t["xout"][i, h * W : (h + 1) * W, :] = row.astype(BF16)
        return carry

    lax.fori_loop(0, 8, leave, 0)
    out_copy = pltpu.make_async_copy(t["xout"], input_o, t["osem"].at[0])
    out_copy.start()
    early.wait()
    gather_a.wait_recv()
    late.wait()
    gather_b.wait_recv()
    out_copy.wait()

    for tag in CHAINS:
        core[tag].wait_send()
    for tag in CHAINS:
        for stage in (seconds, thirds, fourths):
            stage[tag].wait_send()
    for exchange in (
        halo_i3, halo_i4, halo_g4, halo_g3, gather_a, gather_b, early, late,
    ):
        exchange.wait_send()


def results_kernel(
    scale_three, scale_four, input_i, fin_a, fin_b, early, late,
    input_o, k3_o, gain3_o, expand_o, project_o, scale_o, merge_o, patch_o, k4_o, gain4_o,
):
    input_o[...] = input_i[...]
    for c in range(YS * KS):
        q, kk = divmod(c, KS)
        patch_o[:, c * 128 : (c + 1) * 128] = fin_a[c].astype(F32) * scale_four
        project_o[kk * 32 : (kk + 1) * 32, q * 128 : (q + 1) * 128] = (
            fin_b[c, 0:32].astype(F32) * scale_three
        )
        for half in range(2):
            lane = c * 256 + half * 128
            expand_o[:, lane : lane + 128] = (
                fin_b[c, 32 + half * 16 : 48 + half * 16].astype(F32) * scale_three
            )
    for p in range(7):
        k3_o[p] = late[7 * p : 7 * p + 7, :]
        k4_o[p, :, 0:512] = early[7 * p : 7 * p + 7, :]
        k4_o[p, :, 512:1024] = early[56 + 7 * p : 63 + 7 * p, :]
    gain3_o[...] = late[56:57, :]
    scale_o[...] = late[57:58, :]
    merge_o[...] = late[58:59, :]
    gain4_o[:, 0:512] = early[112:113, :]
    gain4_o[:, 512:1024] = early[113:114, :]


def body(
    block_input,
    kernel_three,
    gain_three,
    expand_weight,
    project_weight,
    layer_scale,
    merge_gain,
    patch_weight,
    kernel_four,
    gain_four,
    normed_cotangent,
    residual_cotangent,
):
    devices = lax.axis_size("row") * lax.axis_size("col")
    scale_three = 1.0 / math.sqrt(256 * devices)
    scale_four = 1.0 / math.sqrt(64 * devices)
    table = scratch_table()
    whole = pl.BlockSpec(memory_space=pltpu.VMEM)
    away = pl.BlockSpec(memory_space=pl.ANY)
    flat = lambda v: v.reshape(1, -1)
    moved = pl.pallas_call(
        functools.partial(kernel, scale_three, scale_four, tuple(table)),
        out_shape=(
            jax.ShapeDtypeStruct((8, 32, 512), BF16),
            jax.ShapeDtypeStruct((8, 64, 128), BF16),
            jax.ShapeDtypeStruct((8, 64, 128), BF16),
            jax.ShapeDtypeStruct((128, 512), F32),
            jax.ShapeDtypeStruct((64, 512), F32),
        ),
        in_specs=[away] * 12,
        out_specs=(away,) + (whole,) * 4,
        scratch_shapes=list(table.values()),
        compiler_params=pltpu.CompilerParams(
            collective_id=0, has_side_effects=True, vmem_limit_bytes=60 << 20
        ),
        name="block_backward",
    )(
        block_input.reshape(8, 32, 512),
        kernel_three,
        flat(gain_three),
        expand_weight,
        project_weight,
        flat(layer_scale),
        flat(merge_gain),
        patch_weight,
        kernel_four,
        flat(gain_four),
        normed_cotangent.reshape(64, 1024),
        residual_cotangent.reshape(64, 1024),
    )
    shapes = (
        (8, 32, 512), (7, 7, 512), (1, 512), (16, 2048), (64, 512),
        (1, 512), (1, 512), (64, 1024), (7, 7, 1024), (1, 1024),
    )
    outs = pl.pallas_call(
        functools.partial(results_kernel, scale_three, scale_four),
        out_shape=tuple(
            jax.ShapeDtypeStruct(shape, F32 if n else BF16) for n, shape in enumerate(shapes)
        ),
        in_specs=[whole] * 5,
        out_specs=(whole,) * 10,
        compiler_params=pltpu.CompilerParams(vmem_limit_bytes=16 << 20),
        name="results",
    )(*moved)
    outs = list(outs)
    outs[0] = outs[0].reshape(1, 8, 32, 512)
    for n in (2, 5, 6, 9):
        outs[n] = outs[n].reshape(-1)
    return tuple(outs)


def solution(mesh):
    pixels = P(None, "row", "col", None)
    return jax.shard_map(
        body,
        mesh=mesh,
        in_specs=(pixels,) + (P(),) * 9 + (pixels, pixels),
        out_specs=(pixels, P(), P(), P("row", None), P("row", None), P(), P(), P("row", None), P(), P()),
        check_vma=False,
    )
```
